256 devices in a mesh: ctx: 32 (over x_lo, z, core), head: 8 (over x_hi, y).
Axes of the slice: x: 4 (x_hi: 2, x_lo: 2; x = x_hi * 2 + x_lo), y: 4, z: 8, core: 2. Of those that a mesh axis runs over, the one named last changes fastest.
Arguments:
- queries: bfloat16 [512, 4096], P('ctx', 'head'), may hold values from -1500 to 1500
- cache_keys: bfloat16 [131072, 2048], P('ctx', 'head'), may hold values from -15 to 15
- prefix_cache_values: bfloat16 [131072, 2048], P('ctx', 'head'), may hold values from -6 to 6
- incoming_keys: bfloat16 [512, 2048], P('ctx', 'head'), may hold values from -15 to 15
- incoming_values: bfloat16 [512, 2048], P('ctx', 'head'), may hold values from -6 to 6
Outputs:
- attended: bfloat16 [512, 4096], P('ctx', 'head')
The draws below stay inside these ranges and needn't reach their ends.
All inputs are finite; a program needn't handle non-finite values.
Results may differ from the reference program's by a relative error of at most 0.005.
Values may be sent and summed in bfloat16 or wider, within the bound.
No kernel may reach another device: no remote copies, remote signals or barrier semaphores. Data moves between devices by JAX's collectives and lax.ppermute only.
A program may use at most 64 MiB of HBM per device.

```python
import jax
import jax.numpy as jnp
from jax import lax

QUERY_HEAD_COUNT = 32
KEY_VALUE_HEADS = 16
HEAD_SIZE = 128
PREFIX_TOKENS = 131072
NEW_TOKEN_COUNT = 512


def chosen_pairs(key):
    picker = jax.random.fold_in(key, 12)
    first = jax.random.randint(jax.random.fold_in(picker, 1), (16,), 0, PREFIX_TOKENS)
    second = (first + PREFIX_TOKENS // 2) % PREFIX_TOKENS
    query_rows = jax.random.randint(jax.random.fold_in(picker, 2), (16,), 0, NEW_TOKEN_COUNT)
    current_query_head = jax.random.randint(jax.random.fold_in(picker, 3), (16,), 0, QUERY_HEAD_COUNT)
    strength = jax.random.uniform(jax.random.fold_in(picker, 4), (16,), jnp.float32, 1.8, 4.5)
    return (first, second, query_rows, current_query_head, strength)


def base_keys(key):
    sampled_inputs = 2.5 * jax.random.truncated_normal(jax.random.fold_in(key, 11), -6.0, 6.0, (PREFIX_TOKENS, KEY_VALUE_HEADS * HEAD_SIZE), jnp.float32)
    first, second, query_rows, current_query_head, strength = chosen_pairs(key)
    sampled_inputs = sampled_inputs.at[second].set(0.99 * sampled_inputs[first])
    return sampled_inputs


def draw_cache_keys(key, part):
    return base_keys(key).astype(jnp.bfloat16)


def draw_queries(key, part):
    sampled_inputs = jax.random.truncated_normal(jax.random.fold_in(key, 13), -6.0, 6.0, (NEW_TOKEN_COUNT, QUERY_HEAD_COUNT * HEAD_SIZE), jnp.float32)
    key_table = base_keys(key).astype(jnp.bfloat16).astype(jnp.float32)
    first, second, query_rows, current_query_head, strength = chosen_pairs(key)
    key_value_head = current_query_head // (QUERY_HEAD_COUNT // KEY_VALUE_HEADS)
    offsets = jnp.arange(HEAD_SIZE, dtype=jnp.int32)
    key_cols = key_value_head[:, None] * HEAD_SIZE + offsets[None, :]
    picked = key_table[first[:, None], key_cols] * strength[:, None]
    query_cols = current_query_head[:, None] * HEAD_SIZE + offsets[None, :]
    sampled_inputs = sampled_inputs.at[query_rows[:, None], query_cols].set(picked)
    return sampled_inputs.astype(jnp.bfloat16)


def levels(own_key, dims, shards, least, largest):
    gain, own = 1.0, jax.random.fold_in(own_key, 6)
    for dim, parts in shards:
        steps = jnp.exp(jax.random.uniform(jax.random.fold_in(own, dim), (parts,), jnp.float32, least / len(shards), largest / len(shards)))
        gain = gain * jnp.repeat(steps, dims[dim] // parts).reshape([-1 if axis == dim else 1 for axis in range(len(dims))])
    return gain


def scatter_about(rng, extent, spread, bound, shards=(), kind=jnp.bfloat16):
    drawn = jax.random.normal(rng, extent, jnp.float32) * spread
    if len(shards) > 0:
        drawn = levels(rng, extent, shards, -0.22, 0.18) * drawn
    return jnp.clip(drawn, min=-bound, max=bound).astype(kind)


def setup_inputs(seed: int = 0) -> dict:
    splits = jax.random.split(jax.random.key(seed), 6)
    return {
        "queries": draw_queries(jax.random.fold_in(splits[5], 71), 0),
        "cache_keys": draw_cache_keys(jax.random.fold_in(splits[5], 71), 0),
        "prefix_cache_values": scatter_about(splits[2], (PREFIX_TOKENS, KEY_VALUE_HEADS * HEAD_SIZE), 1.0, 6.0, ((0, 32), (1, 8))),
        "incoming_keys": scatter_about(splits[3], (NEW_TOKEN_COUNT, KEY_VALUE_HEADS * HEAD_SIZE), 2.5, 15.0, ((0, 32), (1, 8))),
        "incoming_values": scatter_about(splits[4], (NEW_TOKEN_COUNT, KEY_VALUE_HEADS * HEAD_SIZE), 1.0, 6.0, ((0, 32), (1, 8))),
    }


score_scale = 168.0 ** -0.5


def prefix_step(state, key_block, query_heads):
    out_acc, row_max, row_sum = state
    block_keys, block_values = key_block
    scores = jnp.einsum("gqd,kd->gqk", query_heads.astype(jnp.float32), block_keys.astype(jnp.float32)) * score_scale
    new_max = jnp.maximum(row_max, jnp.max(scores, axis=-1))
    decay = jnp.exp(row_max - new_max)
    probs = jnp.exp(scores - new_max[..., None])
    row_sum = row_sum * decay + jnp.sum(probs, axis=-1)
    rounded = lax.optimization_barrier(probs.astype(jnp.bfloat16)).astype(jnp.float32)
    out_acc = out_acc * decay[..., None] + jnp.einsum("gqk,kd->gqd", rounded, block_values.astype(jnp.float32))
    return (out_acc, new_max, row_sum), None


def one_head(operands):
    query_heads, head_keys, head_values, fresh_keys, fresh_values = operands
    group_size, total_rows, _ = query_heads.shape
    block_size = min(512, head_keys.shape[0])
    count = head_keys.shape[0] // block_size
    blocks = (head_keys.reshape(count, block_size, HEAD_SIZE), head_values.reshape(count, block_size, HEAD_SIZE))
    init = (jnp.zeros((group_size, total_rows, HEAD_SIZE), jnp.float32),
            jnp.full((group_size, total_rows), -1e30, jnp.float32),
            jnp.zeros((group_size, total_rows), jnp.float32))
    (out_acc, row_max, row_sum), _ = lax.scan(lambda state, key_block: prefix_step(state, key_block, query_heads), init, blocks)
    scores = jnp.einsum("gqd,kd->gqk", query_heads.astype(jnp.float32), fresh_keys.astype(jnp.float32)) * score_scale
    positions = jnp.arange(total_rows, dtype=jnp.int32)
    causal_mask = positions[None, :] <= positions[:, None]
    scores = jnp.where(causal_mask[None], scores, -1e30)
    fresh_max = jnp.max(scores, axis=-1)
    fresh_probs = jnp.where(causal_mask[None], jnp.exp(scores - fresh_max[..., None]), 0.0)
    fresh_sum = jnp.sum(fresh_probs, axis=-1)
    rounded = lax.optimization_barrier(fresh_probs.astype(jnp.bfloat16)).astype(jnp.float32)
    fresh_out = jnp.einsum("gqk,kd->gqd", rounded, fresh_values.astype(jnp.float32))
    merged_max = jnp.maximum(row_max, fresh_max)
    old_weight = jnp.exp(row_max - merged_max)
    new_weight = jnp.exp(fresh_max - merged_max)
    numer = out_acc * old_weight[..., None] + fresh_out * new_weight[..., None]
    denom = row_sum * old_weight + fresh_sum * new_weight
    return (numer / denom[..., None]).astype(jnp.bfloat16)


def reference(queries, cache_keys, prefix_cache_values, incoming_keys, incoming_values):
    total_rows = queries.shape[0]
    kv_heads = cache_keys.shape[1] // HEAD_SIZE
    group_size = queries.shape[1] // cache_keys.shape[1]
    query_heads = queries.reshape(total_rows, kv_heads, group_size, HEAD_SIZE).transpose(1, 2, 0, 3)
    head_keys = cache_keys.reshape(-1, kv_heads, HEAD_SIZE).transpose(1, 0, 2)
    head_values = prefix_cache_values.reshape(-1, kv_heads, HEAD_SIZE).transpose(1, 0, 2)
    fresh_keys = incoming_keys.reshape(total_rows, kv_heads, HEAD_SIZE).transpose(1, 0, 2)
    fresh_values = incoming_values.reshape(total_rows, kv_heads, HEAD_SIZE).transpose(1, 0, 2)
    outputs = lax.map(one_head, (query_heads, head_keys, head_values, fresh_keys, fresh_values))
    return outputs.transpose(2, 0, 1, 3).reshape(total_rows, -1)
```

```python
import functools
import math

import jax
import jax.numpy as jnp
from jax import lax
from jax.experimental import pallas as pl
from jax.experimental.pallas import tpu as pltpu
from jax.sharding import Mesh
from jax.sharding import PartitionSpec as P

HEAD = 128
LANES = 128
LOG2_SCALE = 168.0**-0.5 * math.log2(math.e)
NEG = -1e30
KEY_BLOCK = 2048
ROW_BLOCK = 256
STATS = 8

f32 = jnp.float32
bf16 = jnp.bfloat16

VMEM_LIMIT = 48 << 20


def scores_of(a, b):
    return lax.dot_general(a, b, (((1,), (1,)), ((), ())), preferred_element_type=f32)


def split_three(value):
    high = value.astype(bf16)
    rest = value - high.astype(f32)
    middle = rest.astype(bf16)
    low = (rest - middle.astype(f32)).astype(bf16)
    return high.astype(f32), middle.astype(f32), low.astype(f32)


def packed_stats(m, l):
    pieces = (*split_three(m), *split_three(l))
    n = m.shape[0]
    row = lax.broadcasted_iota(jnp.int32, (n, STATS, LANES), 1)
    out = jnp.zeros((n, STATS, LANES), f32)
    for k, piece in enumerate(pieces):
        out = jnp.where(row == k, jnp.broadcast_to(piece[:, None, :], out.shape), out)
    return out.astype(bf16)


def unpacked_stats(stats):
    s = stats.astype(f32)
    m = (s[:, 2] + s[:, 1]) + s[:, 0]
    l = (s[:, 5] + s[:, 4]) + s[:, 3]
    return m, l


def attend_kernel(heads, place_ref, q_ref, k_ref, v_ref, nk_ref, nv_ref, o_ref, s0, s1):
    tokens = q_ref.shape[0]
    own = nk_ref.shape[0]
    dests = tokens // own
    rows = 2 * tokens
    prefix = k_ref.shape[0]
    blocks = prefix // KEY_BLOCK
    chunks = rows // ROW_BLOCK
    sb = (s0, s1)
    row = lax.broadcasted_iota(jnp.int32, (rows, LANES), 0)
    col = lax.broadcasted_iota(jnp.int32, (rows, LANES), 1)
    token = row % tokens
    position = ((token // own) * 2 + place_ref[1]) * own + token % own
    seen = (col < own) & (position >= place_ref[0] + col)
    maxima = jnp.zeros((dests, own, LANES), f32)
    sums = jnp.zeros((dests, own, LANES), f32)
    at = lax.broadcasted_iota(jnp.int32, (dests, own, LANES), 1)
    lane = lax.broadcasted_iota(jnp.int32, (dests, own, LANES), 2)
    ones = jnp.ones((KEY_BLOCK, LANES), bf16)
    pad = jnp.zeros((LANES - own, HEAD), bf16)
    work = []
    for h in heads:
        for i in range(blocks):
            work.append((h, i))

    queries = {}
    for n, h in enumerate(heads):
        base = 2 * HEAD * h
        queries[h] = jnp.concatenate(
            [q_ref[:, base : base + HEAD], q_ref[:, base + HEAD : base + 2 * HEAD]], axis=0
        )

    def score_block(n):
        h, i = work[n]
        keys = k_ref[i * KEY_BLOCK : (i + 1) * KEY_BLOCK, h * HEAD : (h + 1) * HEAD]
        sb[n % 2][...] = scores_of(queries[h], keys)

    score_block(0)
    acc, top = None, None
    for n, (h, i) in enumerate(work):
        mine = slice(h * HEAD, (h + 1) * HEAD)
        if n + 1 < len(work):
            score_block(n + 1)
        if i == 0:
            keys = jnp.concatenate([nk_ref[:, mine], pad], axis=0)
            vals = jnp.concatenate([nv_ref[:, mine], pad], axis=0)
            s = jnp.where(seen, scores_of(queries[h], keys), NEG)
            m = jnp.broadcast_to(jnp.max(s, axis=1, keepdims=True), s.shape)
            p = jnp.where(seen, jnp.exp2((s - m) * LOG2_SCALE), 0.0).astype(bf16)
            vals = jnp.concatenate([vals, ones[:LANES]], axis=1)
            a = jnp.dot(p, vals, preferred_element_type=f32)
            acc = [a[r * ROW_BLOCK : (r + 1) * ROW_BLOCK] for r in range(chunks)]
            top = [m[r * ROW_BLOCK : (r + 1) * ROW_BLOCK] for r in range(chunks)]
        vals = v_ref[i * KEY_BLOCK : (i + 1) * KEY_BLOCK, mine]
        vals = jnp.concatenate([vals, ones], axis=1)
        for r in range(chunks):
            s = sb[n % 2][r * ROW_BLOCK : (r + 1) * ROW_BLOCK]
            m = jnp.maximum(top[r], jnp.max(s, axis=1, keepdims=True))
            p = jnp.exp2((s - jnp.tile(m, (1, KEY_BLOCK // LANES))) * LOG2_SCALE)
            decay = jnp.exp2((top[r] - m) * LOG2_SCALE)
            acc[r] = acc[r] * jnp.tile(decay, (1, 2)) + jnp.dot(
                p.astype(bf16), vals, preferred_element_type=f32
            )
            top[r] = m
        if i == blocks - 1:
            slot = heads.index(h)
            whole = jnp.concatenate(acc, axis=0)
            whole_top = jnp.concatenate(top, axis=0)
            for g in range(2):
                part = whole[g * tokens : (g + 1) * tokens]
                o_ref[:, (slot * 2 + g) * own : (slot * 2 + g + 1) * own, :] = (
                    part[:, :HEAD].reshape(dests, own, HEAD).astype(bf16)
                )
                pick = lane == (h * 2 + g) * own + at
                maxima = maxima + jnp.where(
                    pick, whole_top[g * tokens : (g + 1) * tokens].reshape(dests, own, LANES), 0.0
                )
                sums = sums + jnp.where(pick, part[:, HEAD:].reshape(dests, own, LANES), 0.0)
    o_ref[:, len(heads) * 2 * own :, :] = packed_stats(jnp.sum(maxima, axis=1), jnp.sum(sums, axis=1))


def attend(heads, place, queries, keys, values, new_keys, new_values):
    tokens, own = queries.shape[0], new_keys.shape[0]
    rows, prefix = 2 * tokens, keys.shape[0]
    whole = pl.BlockSpec(memory_space=pltpu.VMEM)
    return pl.pallas_call(
        functools.partial(attend_kernel, heads),
        in_specs=[pl.BlockSpec(memory_space=pltpu.SMEM), whole, whole, whole, whole, whole],
        out_specs=whole,
        out_shape=jax.ShapeDtypeStruct(
            (tokens // own, len(heads) * 2 * own + STATS, HEAD), bf16
        ),
        scratch_shapes=[pltpu.VMEM((rows, KEY_BLOCK), f32)] * 2,
        compiler_params=pltpu.CompilerParams(vmem_limit_bytes=VMEM_LIMIT),
        cost_estimate=pl.CostEstimate(
            flops=len(heads) * 8 * rows * prefix * HEAD,
            bytes_accessed=len(heads) * prefix * HEAD * 4,
            transcendentals=len(heads) * rows * prefix,
        ),
        name="attend",
    )(place, queries, keys, values, new_keys, new_values)


def columns_of(rows):
    n = rows.shape[0]
    if n < LANES:
        rows = jnp.concatenate([rows, jnp.zeros((LANES - n, LANES), f32)], axis=0)
    return jnp.transpose(rows)


def merge_kernel(pairs, a0_ref, a1_ref, b_ref, o_ref):
    n, half = a0_ref.shape[0], pairs // 2
    stats = a0_ref[:, half:, :].astype(f32) + a1_ref[:, half:, :].astype(f32)
    ma, la = unpacked_stats(stats)
    mb, lb = unpacked_stats(b_ref[:, pairs:, :])
    m = jnp.maximum(ma, mb)
    wa, wb = jnp.exp2((ma - m) * LOG2_SCALE), jnp.exp2((mb - m) * LOG2_SCALE)
    o_ref[:, pairs:, :] = packed_stats(m, la * wa + lb * wb)
    cols = columns_of(jnp.concatenate([wa, wb], axis=0))
    for d in range(n):
        for k, a_ref in enumerate((a0_ref, a1_ref)):
            span = slice(k * half, (k + 1) * half)
            mixed = (
                a_ref[d, :half].astype(f32) * cols[span, d : d + 1]
                + b_ref[d, span].astype(f32) * cols[span, n + d : n + d + 1]
            )
            o_ref[d, span] = mixed.astype(bf16)


def merge(a0, a1, b):
    whole = pl.BlockSpec(memory_space=pltpu.VMEM)
    pairs = b.shape[1] - STATS
    return pl.pallas_call(
        functools.partial(merge_kernel, pairs),
        in_specs=[whole] * 3,
        out_specs=whole,
        out_shape=jax.ShapeDtypeStruct(b.shape, bf16),
        name="merge",
    )(a0, a1, b)


def finish_kernel(own, r_ref, o_ref):
    n, pairs = r_ref.shape[0], r_ref.shape[1] - STATS
    m, l = unpacked_stats(r_ref[:, pairs:, :])
    w = jnp.exp2((m - jnp.max(m, axis=0, keepdims=True)) * LOG2_SCALE)
    cols = columns_of(w / jnp.sum(l * w, axis=0, keepdims=True))
    out = r_ref[0, :pairs].astype(f32) * cols[:pairs, 0:1]
    for s in range(1, n):
        out = out + r_ref[s, :pairs].astype(f32) * cols[:pairs, s : s + 1]
    for j in range(pairs // own):
        o_ref[:, j * HEAD : (j + 1) * HEAD] = out[j * own : (j + 1) * own].astype(bf16)


def finish(received, own, width):
    whole = pl.BlockSpec(memory_space=pltpu.VMEM)
    return pl.pallas_call(
        functools.partial(finish_kernel, own),
        in_specs=[whole],
        out_specs=whole,
        out_shape=jax.ShapeDtypeStruct((own, width), bf16),
        name="finish",
    )(received)


PLANE = ("xl", "z")


def exchanged(blocks):
    return lax.all_to_all(blocks, PLANE, split_axis=0, concat_axis=0, tiled=True)


def from_other_core(value):
    return lax.ppermute(value, "c", [(0, 1), (1, 0)])


def shards(queries, cache_keys, prefix_cache_values, incoming_keys, incoming_values):
    own, width = queries.shape
    chips = lax.axis_size("xl") * lax.axis_size("z")
    chip = lax.axis_index("xl") * lax.axis_size("z") + lax.axis_index("z")
    core = lax.axis_index("c")
    first = ((chip * 2 + core) * own).astype(jnp.int32)
    local = (cache_keys, prefix_cache_values, incoming_keys, incoming_values)
    same = exchanged(jnp.broadcast_to(queries, (chips, own, width))).reshape(chips * own, width)
    other = from_other_core(same)
    at_same = jnp.stack([first, core.astype(jnp.int32)])
    at_other = jnp.stack([first, 1 - core.astype(jnp.int32)])
    mine0 = attend((0,), at_same, same, *local)
    theirs = attend((0, 1), at_other, other, *local)
    from_sibling = from_other_core(theirs)
    mine1 = attend((1,), at_same, same, *local)
    merged = merge(mine0, mine1, from_sibling)
    return finish(exchanged(merged), own, width)


def solution(mesh):
    fine = Mesh(mesh.devices.reshape(2, -1, 2, mesh.devices.shape[1]), ("xl", "z", "c", "head"))
    spec = P(("xl", "z", "c"), "head")
    return jax.shard_map(shards, mesh=fine, in_specs=(spec,) * 5, out_specs=spec, check_vma=False)
```

```python
import functools
import math

import jax
import jax.numpy as jnp
from jax import lax
from jax.experimental import pallas as pl
from jax.experimental.pallas import tpu as pltpu
from jax.sharding import Mesh
from jax.sharding import PartitionSpec as P

HEAD = 128
LANES = 128
LOG2_SCALE = 168.0**-0.5 * math.log2(math.e)
NEG = -1e30
KEY_BLOCK = 2048
ROW_BLOCK = 256
STATS = 8

f32 = jnp.float32
bf16 = jnp.bfloat16

ATTEND_VMEM = 32 << 20
SMALL_VMEM = 4 << 20


def scores_of(a, b):
    return lax.dot_general(a, b, (((1,), (1,)), ((), ())), preferred_element_type=f32)


def split_three(value):
    high = value.astype(bf16)
    rest = value - high.astype(f32)
    middle = rest.astype(bf16)
    low = (rest - middle.astype(f32)).astype(bf16)
    return high.astype(f32), middle.astype(f32), low.astype(f32)


def packed_stats(m, l):
    pieces = (*split_three(m), *split_three(l))
    n = m.shape[0]
    row = lax.broadcasted_iota(jnp.int32, (n, STATS, LANES), 1)
    out = jnp.zeros((n, STATS, LANES), f32)
    for k, piece in enumerate(pieces):
        out = jnp.where(row == k, jnp.broadcast_to(piece[:, None, :], out.shape), out)
    return out.astype(bf16)


def unpacked_stats(stats):
    s = stats.astype(f32)
    m = (s[:, 2] + s[:, 1]) + s[:, 0]
    l = (s[:, 5] + s[:, 4]) + s[:, 3]
    return m, l


def attend_kernel(heads, place_ref, q_ref, k_ref, v_ref, nk_ref, nv_ref, o_ref, *rest):
    fetch = len(rest) > 2
    copies = {}
    if fetch:
        k_hbm, v_hbm, nk_hbm, nv_hbm = k_ref, v_ref, nk_ref, nv_ref
        k_ref, v_ref, nk_ref, nv_ref, s0, s1, sems = rest
        kv_heads, per_head = k_hbm.shape[1] // HEAD, k_hbm.shape[0] // KEY_BLOCK
        copies["nk"] = pltpu.make_async_copy(nk_hbm, nk_ref, sems.at[0])
        copies["nv"] = pltpu.make_async_copy(nv_hbm, nv_ref, sems.at[1])
        for h in (*heads, *(h for h in range(kv_heads) if h not in heads)):
            for i in range(per_head):
                for name, source, target in (("k", k_hbm, k_ref), ("v", v_hbm, v_ref)):
                    span = (
                        slice(i * KEY_BLOCK, (i + 1) * KEY_BLOCK),
                        slice(h * HEAD, (h + 1) * HEAD),
                    )
                    copies[name, h, i] = pltpu.make_async_copy(
                        source.at[span], target.at[span], sems.at[len(copies)]
                    )
        for copy in copies.values():
            copy.start()
    else:
        s0, s1 = rest

    def arrived(block):
        if block in copies:
            copies.pop(block).wait()

    tokens = q_ref.shape[0]
    own = nk_ref.shape[0]
    dests = tokens // own
    rows = 2 * tokens
    prefix = k_ref.shape[0]
    blocks = prefix // KEY_BLOCK
    chunks = rows // ROW_BLOCK
    sb = (s0, s1)
    row = lax.broadcasted_iota(jnp.int32, (rows, LANES), 0)
    col = lax.broadcasted_iota(jnp.int32, (rows, LANES), 1)
    token = row % tokens
    position = ((token // own) * 2 + place_ref[1]) * own + token % own
    seen = (col < own) & (position >= place_ref[0] + col)
    maxima = jnp.zeros((dests, own, LANES), f32)
    sums = jnp.zeros((dests, own, LANES), f32)
    at = lax.broadcasted_iota(jnp.int32, (dests, own, LANES), 1)
    lane = lax.broadcasted_iota(jnp.int32, (dests, own, LANES), 2)
    ones = jnp.ones((KEY_BLOCK, LANES), bf16)
    pad = jnp.zeros((LANES - own, HEAD), bf16)
    work = []
    for h in heads:
        for i in range(blocks):
            work.append((h, i))

    queries = {}
    for n, h in enumerate(heads):
        base = 2 * HEAD * h
        queries[h] = jnp.concatenate(
            [q_ref[:, base : base + HEAD], q_ref[:, base + HEAD : base + 2 * HEAD]], axis=0
        )

    def score_block(n):
        h, i = work[n]
        arrived(("k", h, i))
        keys = k_ref[i * KEY_BLOCK : (i + 1) * KEY_BLOCK, h * HEAD : (h + 1) * HEAD]
        sb[n % 2][...] = scores_of(queries[h], keys)

    score_block(0)
    acc, top = None, None
    for n, (h, i) in enumerate(work):
        mine = slice(h * HEAD, (h + 1) * HEAD)
        if n + 1 < len(work):
            score_block(n + 1)
        if i == 0:
            arrived("nk")
            arrived("nv")
            keys = jnp.concatenate([nk_ref[:, mine], pad], axis=0)
            vals = jnp.concatenate([nv_ref[:, mine], pad], axis=0)
            s = jnp.where(seen, scores_of(queries[h], keys), NEG)
            m = jnp.broadcast_to(jnp.max(s, axis=1, keepdims=True), s.shape)
            p = jnp.where(seen, jnp.exp2((s - m) * LOG2_SCALE), 0.0).astype(bf16)
            vals = jnp.concatenate([vals, ones[:LANES]], axis=1)
            a = jnp.dot(p, vals, preferred_element_type=f32)
            acc = [a[r * ROW_BLOCK : (r + 1) * ROW_BLOCK] for r in range(chunks)]
            top = [m[r * ROW_BLOCK : (r + 1) * ROW_BLOCK] for r in range(chunks)]
        arrived(("v", h, i))
        vals = v_ref[i * KEY_BLOCK : (i + 1) * KEY_BLOCK, mine]
        vals = jnp.concatenate([vals, ones], axis=1)
        for r in range(chunks):
            s = sb[n % 2][r * ROW_BLOCK : (r + 1) * ROW_BLOCK]
            m = jnp.maximum(top[r], jnp.max(s, axis=1, keepdims=True))
            p = jnp.exp2((s - jnp.tile(m, (1, KEY_BLOCK // LANES))) * LOG2_SCALE)
            decay = jnp.exp2((top[r] - m) * LOG2_SCALE)
            acc[r] = acc[r] * jnp.tile(decay, (1, 2)) + jnp.dot(
                p.astype(bf16), vals, preferred_element_type=f32
            )
            top[r] = m
        if i == blocks - 1:
            slot = heads.index(h)
            whole = jnp.concatenate(acc, axis=0)
            whole_top = jnp.concatenate(top, axis=0)
            for g in range(2):
                part = whole[g * tokens : (g + 1) * tokens]
                o_ref[:, (slot * 2 + g) * own : (slot * 2 + g + 1) * own, :] = (
                    part[:, :HEAD].reshape(dests, own, HEAD).astype(bf16)
                )
                pick = lane == (h * 2 + g) * own + at
                maxima = maxima + jnp.where(
                    pick, whole_top[g * tokens : (g + 1) * tokens].reshape(dests, own, LANES), 0.0
                )
                sums = sums + jnp.where(pick, part[:, HEAD:].reshape(dests, own, LANES), 0.0)
    o_ref[:, len(heads) * 2 * own :, :] = packed_stats(
        jnp.sum(maxima, axis=1), jnp.sum(sums, axis=1)
    )
    for block in tuple(copies):
        arrived(block)


def attend(heads, place, queries, keys, values, new_keys, new_values, fetch=False):
    tokens, own = queries.shape[0], new_keys.shape[0]
    rows, prefix = 2 * tokens, keys.shape[0]
    whole = pl.BlockSpec(memory_space=pltpu.VMEM)
    cache = pl.BlockSpec(memory_space=pltpu.HBM) if fetch else whole
    out_shape = [
        jax.ShapeDtypeStruct((tokens // own, len(heads) * 2 * own + STATS, HEAD), bf16)
    ]
    scratch = [pltpu.VMEM((rows, KEY_BLOCK), f32)] * 2
    if fetch:
        moved = (keys, values, new_keys, new_values)
        out_shape += [jax.ShapeDtypeStruct(a.shape, a.dtype) for a in moved]
        blocks = 2 * (keys.shape[1] // HEAD) * (prefix // KEY_BLOCK)
        scratch.append(pltpu.SemaphoreType.DMA((blocks + 2,)))
        keys, values, new_keys, new_values = (
            pltpu.with_memory_space_constraint(a, pltpu.HBM) for a in moved
        )
    return pl.pallas_call(
        functools.partial(attend_kernel, heads),
        in_specs=[pl.BlockSpec(memory_space=pltpu.SMEM), whole, cache, cache, cache, cache],
        out_specs=[whole] * len(out_shape),
        out_shape=out_shape,
        scratch_shapes=scratch,
        compiler_params=pltpu.CompilerParams(vmem_limit_bytes=ATTEND_VMEM),
        cost_estimate=pl.CostEstimate(
            flops=len(heads) * 8 * rows * prefix * HEAD,
            bytes_accessed=len(heads) * prefix * HEAD * 4,
            transcendentals=len(heads) * rows * prefix,
        ),
        name="attend",
    )(place, queries, keys, values, new_keys, new_values)


def columns_of(rows):
    n = rows.shape[0]
    if n < LANES:
        rows = jnp.concatenate([rows, jnp.zeros((LANES - n, LANES), f32)], axis=0)
    return jnp.transpose(rows)


def merge_kernel(pairs, a0_ref, a1_ref, b_ref, o_ref):
    n, half = a0_ref.shape[0], pairs // 2
    stats = a0_ref[:, half:, :].astype(f32) + a1_ref[:, half:, :].astype(f32)
    ma, la = unpacked_stats(stats)
    mb, lb = unpacked_stats(b_ref[:, pairs:, :])
    m = jnp.maximum(ma, mb)
    wa, wb = jnp.exp2((ma - m) * LOG2_SCALE), jnp.exp2((mb - m) * LOG2_SCALE)
    o_ref[:, pairs:, :] = packed_stats(m, la * wa + lb * wb)
    cols = columns_of(jnp.concatenate([wa, wb], axis=0))
    for d in range(n):
        for k, a_ref in enumerate((a0_ref, a1_ref)):
            span = slice(k * half, (k + 1) * half)
            mixed = (
                a_ref[d, :half].astype(f32) * cols[span, d : d + 1]
                + b_ref[d, span].astype(f32) * cols[span, n + d : n + d + 1]
            )
            o_ref[d, span] = mixed.astype(bf16)


def merge(a0, a1, b):
    whole = pl.BlockSpec(memory_space=pltpu.VMEM)
    pairs = b.shape[1] - STATS
    return pl.pallas_call(
        functools.partial(merge_kernel, pairs),
        in_specs=[whole] * 3,
        out_specs=whole,
        out_shape=jax.ShapeDtypeStruct(b.shape, bf16),
        compiler_params=pltpu.CompilerParams(vmem_limit_bytes=SMALL_VMEM),
        name="merge",
    )(a0, a1, b)


def finish_kernel(own, r_ref, o_ref):
    n, pairs = r_ref.shape[0], r_ref.shape[1] - STATS
    m, l = unpacked_stats(r_ref[:, pairs:, :])
    w = jnp.exp2((m - jnp.max(m, axis=0, keepdims=True)) * LOG2_SCALE)
    cols = columns_of(w / jnp.sum(l * w, axis=0, keepdims=True))
    out = r_ref[0, :pairs].astype(f32) * cols[:pairs, 0:1]
    for s in range(1, n):
        out = out + r_ref[s, :pairs].astype(f32) * cols[:pairs, s : s + 1]
    for j in range(pairs // own):
        o_ref[:, j * HEAD : (j + 1) * HEAD] = out[j * own : (j + 1) * own].astype(bf16)


def finish(received, own, width):
    whole = pl.BlockSpec(memory_space=pltpu.VMEM)
    return pl.pallas_call(
        functools.partial(finish_kernel, own),
        in_specs=[whole],
        out_specs=whole,
        out_shape=jax.ShapeDtypeStruct((own, width), bf16),
        compiler_params=pltpu.CompilerParams(vmem_limit_bytes=SMALL_VMEM),
        name="finish",
    )(received)


PLANE = ("xl", "z")


def exchanged(blocks):
    return lax.all_to_all(blocks, PLANE, split_axis=0, concat_axis=0, tiled=True)


def from_other_core(value):
    return lax.ppermute(value, "c", [(0, 1), (1, 0)])


def shards(queries, cache_keys, prefix_cache_values, incoming_keys, incoming_values):
    own, width = queries.shape
    chips = lax.axis_size("xl") * lax.axis_size("z")
    chip = lax.axis_index("xl") * lax.axis_size("z") + lax.axis_index("z")
    core = lax.axis_index("c")
    first = ((chip * 2 + core) * own).astype(jnp.int32)
    local = (cache_keys, prefix_cache_values, incoming_keys, incoming_values)
    same = exchanged(jnp.broadcast_to(queries, (chips, own, width))).reshape(chips * own, width)
    other = from_other_core(same)
    at_same = jnp.stack([first, core.astype(jnp.int32)])
    at_other = jnp.stack([first, 1 - core.astype(jnp.int32)])
    mine0, *local = attend((0,), at_same, same, *local, fetch=True)
    (theirs,) = attend((0, 1), at_other, other, *local)
    from_sibling = from_other_core(theirs)
    at_same, theirs = lax.optimization_barrier((at_same, theirs))
    (mine1,) = attend((1,), at_same, same, *local)
    merged = merge(mine0, mine1, from_sibling)
    return finish(exchanged(merged), own, width)


def solution(mesh):
    fine = Mesh(mesh.devices.reshape(2, -1, 2, mesh.devices.shape[1]), ("xl", "z", "c", "head"))
    spec = P(("xl", "z", "c"), "head")
    return jax.shard_map(shards, mesh=fine, in_specs=(spec,) * 5, out_specs=spec, check_vma=False)
```

```python
import functools
import math

import jax
import jax.numpy as jnp
from jax import lax
from jax.experimental import pallas as pl
from jax.experimental.pallas import tpu as pltpu
from jax.sharding import Mesh
from jax.sharding import PartitionSpec as P

HEAD = 128
LANES = 128
LOG2_SCALE = 168.0**-0.5 * math.log2(math.e)
NEG = -1e30
KEY_BLOCK = 2048
ROW_BLOCK = 256
STATS = 8
PARTS = 4

f32 = jnp.float32
bf16 = jnp.bfloat16

ATTEND_VMEM = 32 << 20
SMALL_VMEM = 4 << 20


def scores_of(a, b):
    return lax.dot_general(a, b, (((1,), (1,)), ((), ())), preferred_element_type=f32)


def split_three(value):
    high = value.astype(bf16)
    rest = value - high.astype(f32)
    middle = rest.astype(bf16)
    low = (rest - middle.astype(f32)).astype(bf16)
    return high.astype(f32), middle.astype(f32), low.astype(f32)


def packed_stats(m, l):
    pieces = (*split_three(m), *split_three(l))
    n = m.shape[0]
    row = lax.broadcasted_iota(jnp.int32, (n, STATS, LANES), 1)
    out = jnp.zeros((n, STATS, LANES), f32)
    for k, piece in enumerate(pieces):
        out = jnp.where(row == k, jnp.broadcast_to(piece[:, None, :], out.shape), out)
    return out.astype(bf16)


def unpacked_stats(stats):
    s = stats.astype(f32)
    m = (s[:, 2] + s[:, 1]) + s[:, 0]
    l = (s[:, 5] + s[:, 4]) + s[:, 3]
    return m, l


def load_kernel(k_ref, v_ref, nk_ref, nv_ref, k_out, v_out, nk_out, nv_out, sems):
    pairs = [(nk_ref, nk_out), (nv_ref, nv_out)]
    step = k_ref.shape[0] // PARTS
    for p in range(PARTS):
        span = pl.ds(p * step, step)
        pairs.append((k_ref.at[span], k_out.at[span]))
        pairs.append((v_ref.at[span, pl.ds(0, HEAD)], v_out.at[span]))
    copies = [
        pltpu.make_async_copy(source, target, sems.at[n])
        for n, (source, target) in enumerate(pairs)
    ]
    for copy in copies:
        copy.start()
    for copy in copies:
        copy.wait()


def loaded(keys, values, new_keys, new_values):
    arrays = (keys, values, new_keys, new_values)
    outs = [jax.ShapeDtypeStruct(a.shape, a.dtype) for a in arrays]
    outs[1] = jax.ShapeDtypeStruct((values.shape[0], HEAD), values.dtype)
    return pl.pallas_call(
        load_kernel,
        in_specs=[pl.BlockSpec(memory_space=pltpu.HBM)] * len(arrays),
        out_specs=[pl.BlockSpec(memory_space=pltpu.VMEM)] * len(arrays),
        out_shape=outs,
        scratch_shapes=[pltpu.SemaphoreType.DMA((2 * PARTS + 2,))],
        compiler_params=pltpu.CompilerParams(vmem_limit_bytes=SMALL_VMEM),
        cost_estimate=pl.CostEstimate(
            flops=0,
            bytes_accessed=sum(2 * a.size * a.dtype.itemsize for a in outs),
            transcendentals=0,
        ),
        name="load",
    )(*(pltpu.with_memory_space_constraint(a, pltpu.HBM) for a in arrays))


def attend_kernel(same_x, same_c, q_ref, k_ref, v0_ref, v1_ref, nk_ref, nv_ref, o_ref, *rest):
    copies = {}
    if len(rest) > 2:
        v_hbm, (v1_ref, s0, s1, sems) = v1_ref, rest
        for i in range(v_hbm.shape[0] // KEY_BLOCK):
            span = pl.ds(i * KEY_BLOCK, KEY_BLOCK)
            copies[1, i] = pltpu.make_async_copy(
                v_hbm.at[span, pl.ds(HEAD, HEAD)], v1_ref.at[span], sems.at[i]
            )
        for copy in copies.values():
            copy.start()
    else:
        s0, s1 = rest
    values = (v0_ref, v1_ref)
    tokens = q_ref.shape[0]
    own = nk_ref.shape[0]
    dests = tokens // own
    rows = 2 * tokens
    kv_heads = k_ref.shape[1] // HEAD
    blocks = k_ref.shape[0] // KEY_BLOCK
    chunks = rows // ROW_BLOCK
    x, z, c = lax.axis_index("xl"), lax.axis_index("z"), lax.axis_index("c")
    first = ((x * dests + z) * 2 + c) * own
    from_x, from_c = (x if same_x else 1 - x), (c if same_c else 1 - c)
    sb = (s0, s1)
    row = lax.broadcasted_iota(jnp.int32, (rows, LANES), 0)
    col = lax.broadcasted_iota(jnp.int32, (rows, LANES), 1)
    token = row % tokens
    position = ((from_x * dests + token // own) * 2 + from_c) * own + token % own
    seen = (col < own) & (position >= first + col)
    at = lax.broadcasted_iota(jnp.int32, (dests, own, LANES), 1)
    lane = lax.broadcasted_iota(jnp.int32, (dests, own, LANES), 2)
    ones = jnp.ones((KEY_BLOCK, LANES), bf16)
    pad = jnp.zeros((LANES - own, HEAD), bf16)
    work = [(h, i) for h in range(kv_heads) for i in range(blocks)]
    queries = [
        jnp.concatenate(
            [q_ref[:, (2 * h + g) * HEAD : (2 * h + g + 1) * HEAD] for g in range(2)], axis=0
        )
        for h in range(kv_heads)
    ]

    def score_block(n):
        h, i = work[n]
        keys = k_ref[i * KEY_BLOCK : (i + 1) * KEY_BLOCK, h * HEAD : (h + 1) * HEAD]
        sb[n % 2][...] = scores_of(queries[h], keys)

    score_block(0)
    maxima = jnp.zeros((dests, own, LANES), f32)
    sums = jnp.zeros((dests, own, LANES), f32)
    for n, (h, i) in enumerate(work):
        mine = slice(h * HEAD, (h + 1) * HEAD)
        if n + 1 < len(work):
            score_block(n + 1)
        if i == 0:
            keys = jnp.concatenate([nk_ref[:, mine], pad], axis=0)
            vals = jnp.concatenate([nv_ref[:, mine], pad], axis=0)
            s = jnp.where(seen, scores_of(queries[h], keys), NEG)
            m = jnp.broadcast_to(jnp.max(s, axis=1, keepdims=True), s.shape)
            p = jnp.where(seen, jnp.exp2((s - m) * LOG2_SCALE), 0.0).astype(bf16)
            vals = jnp.concatenate([vals, ones[:LANES]], axis=1)
            a = jnp.dot(p, vals, preferred_element_type=f32)
            acc = [a[r * ROW_BLOCK : (r + 1) * ROW_BLOCK] for r in range(chunks)]
            top = [m[r * ROW_BLOCK : (r + 1) * ROW_BLOCK] for r in range(chunks)]
        if (h, i) in copies:
            copies[h, i].wait()
        vals = jnp.concatenate([values[h][i * KEY_BLOCK : (i + 1) * KEY_BLOCK], ones], axis=1)
        for r in range(chunks):
            s = sb[n % 2][r * ROW_BLOCK : (r + 1) * ROW_BLOCK]
            m = jnp.maximum(top[r], jnp.max(s, axis=1, keepdims=True))
            p = jnp.exp2((s - jnp.tile(m, (1, KEY_BLOCK // LANES))) * LOG2_SCALE)
            decay = jnp.exp2((top[r] - m) * LOG2_SCALE)
            acc[r] = acc[r] * jnp.tile(decay, (1, 2)) + jnp.dot(
                p.astype(bf16), vals, preferred_element_type=f32
            )
            top[r] = m
        if i == blocks - 1:
            whole, whole_top = jnp.concatenate(acc, axis=0), jnp.concatenate(top, axis=0)
            for g in range(2):
                slot = h * 2 + g
                part = whole[g * tokens : (g + 1) * tokens]
                part_top = whole_top[g * tokens : (g + 1) * tokens]
                o_ref[:, slot * own : (slot + 1) * own, :] = (
                    part[:, :HEAD].reshape(dests, own, HEAD).astype(bf16)
                )
                pick = lane == slot * own + at
                maxima = maxima + jnp.where(pick, part_top.reshape(dests, own, LANES), 0.0)
                sums = sums + jnp.where(pick, part[:, HEAD:].reshape(dests, own, LANES), 0.0)
    o_ref[:, 2 * kv_heads * own :, :] = packed_stats(
        jnp.sum(maxima, axis=1), jnp.sum(sums, axis=1)
    )


def attend(same_x, same_c, queries, keys, first, second, new_keys, new_values, fetch=False):
    (tokens, width), own = queries.shape, new_keys.shape[0]
    rows, prefix = 2 * tokens, keys.shape[0]
    whole = pl.BlockSpec(memory_space=pltpu.VMEM)
    specs = [whole] * 6
    outs = [
        jax.ShapeDtypeStruct((tokens // own, width // HEAD * own + STATS, HEAD), bf16)
    ]
    scratch = [pltpu.VMEM((rows, KEY_BLOCK), f32)] * 2
    if fetch:
        specs[3] = pl.BlockSpec(memory_space=pltpu.HBM)
        outs.append(jax.ShapeDtypeStruct(first.shape, first.dtype))
        scratch.append(pltpu.SemaphoreType.DMA((prefix // KEY_BLOCK,)))
        second = pltpu.with_memory_space_constraint(second, pltpu.HBM)
    return pl.pallas_call(
        functools.partial(attend_kernel, same_x, same_c),
        in_specs=specs,
        out_specs=[whole] * len(outs),
        out_shape=outs,
        scratch_shapes=scratch,
        compiler_params=pltpu.CompilerParams(vmem_limit_bytes=ATTEND_VMEM),
        cost_estimate=pl.CostEstimate(
            flops=4 * tokens * width * prefix,
            bytes_accessed=4 * prefix * keys.shape[1],
            transcendentals=tokens * width // HEAD * prefix,
        ),
        name="attend",
    )(queries, keys, first, second, new_keys, new_values)


def columns_of(rows):
    n = rows.shape[0]
    if n < LANES:
        rows = jnp.concatenate([rows, jnp.zeros((LANES - n, LANES), f32)], axis=0)
    return jnp.transpose(rows)


def merge_kernel(here_ref, here_sib_ref, there_ref, there_sib_ref, o_ref):
    n, pairs = here_ref.shape[0], here_ref.shape[1] - STATS
    x = lax.axis_index("xl")
    for at, a_ref, b_ref in (
        (x * n, here_ref, here_sib_ref),
        ((1 - x) * n, there_ref, there_sib_ref),
    ):
        ma, la = unpacked_stats(a_ref[:, pairs:, :])
        mb, lb = unpacked_stats(b_ref[:, pairs:, :])
        m = jnp.maximum(ma, mb)
        wa, wb = jnp.exp2((ma - m) * LOG2_SCALE), jnp.exp2((mb - m) * LOG2_SCALE)
        o_ref[pl.ds(at, n), pairs:, :] = packed_stats(m, la * wa + lb * wb)
        cols = columns_of(jnp.concatenate([wa, wb], axis=0))
        for d in range(n):
            mixed = (
                a_ref[d, :pairs].astype(f32) * cols[:pairs, d : d + 1]
                + b_ref[d, :pairs].astype(f32) * cols[:pairs, n + d : n + d + 1]
            )
            o_ref[at + d, :pairs] = mixed.astype(bf16)


def merge(here, here_sib, there, there_sib):
    whole = pl.BlockSpec(memory_space=pltpu.VMEM)
    n, height, _ = here.shape
    return pl.pallas_call(
        merge_kernel,
        in_specs=[whole] * 4,
        out_specs=whole,
        out_shape=jax.ShapeDtypeStruct((2 * n, height, HEAD), bf16),
        compiler_params=pltpu.CompilerParams(vmem_limit_bytes=SMALL_VMEM),
        name="merge",
    )(here, here_sib, there, there_sib)


def finish_kernel(own, r_ref, o_ref):
    n, pairs = r_ref.shape[0], r_ref.shape[1] - STATS
    m, l = unpacked_stats(r_ref[:, pairs:, :])
    w = jnp.exp2((m - jnp.max(m, axis=0, keepdims=True)) * LOG2_SCALE)
    cols = columns_of(w / jnp.sum(l * w, axis=0, keepdims=True))
    out = r_ref[0, :pairs].astype(f32) * cols[:pairs, 0:1]
    for s in range(1, n):
        out = out + r_ref[s, :pairs].astype(f32) * cols[:pairs, s : s + 1]
    for j in range(pairs // own):
        o_ref[:, j * HEAD : (j + 1) * HEAD] = out[j * own : (j + 1) * own].astype(bf16)


def finish(received, own, width):
    whole = pl.BlockSpec(memory_space=pltpu.VMEM)
    return pl.pallas_call(
        functools.partial(finish_kernel, own),
        in_specs=[whole],
        out_specs=whole,
        out_shape=jax.ShapeDtypeStruct((own, width), bf16),
        compiler_params=pltpu.CompilerParams(vmem_limit_bytes=SMALL_VMEM),
        name="finish",
    )(received)


def exchanged(blocks, axes):
    return lax.all_to_all(blocks, axes, split_axis=0, concat_axis=0, tiled=True)


def swapped(value, axis):
    return lax.ppermute(value, axis, [(0, 1), (1, 0)])


def after(value, earlier):
    return lax.optimization_barrier((value, earlier))[0]


def shards(queries, cache_keys, prefix_cache_values, incoming_keys, incoming_values):
    own, width = queries.shape
    column = lax.axis_size("z")
    local = loaded(cache_keys, prefix_cache_values, incoming_keys, incoming_values)
    here = exchanged(jnp.broadcast_to(queries, (column, own, width)), "z")
    here, *local = lax.optimization_barrier((here, *local))
    here = here.reshape(column * own, width)
    here_other = swapped(here, "c")
    there = swapped(here, "xl")
    keys, first, *fresh = local
    part_here, second = attend(
        True, True, here, keys, first, prefix_cache_values, *fresh, fetch=True
    )
    local = (keys, first, second, *fresh)
    there, here_other, part_here = lax.optimization_barrier((there, here_other, part_here))
    there_other = swapped(there, "c")
    (part_here_other,) = attend(True, False, here_other, *local)
    here_sib = swapped(part_here_other, "c")
    (part_there_other,) = attend(False, False, after(there_other, part_here_other), *local)
    there_sib = swapped(part_there_other, "c")
    (part_there,) = attend(False, True, after(there, part_there_other), *local)
    merged = merge(part_here, here_sib, part_there, there_sib)
    return finish(exchanged(merged, ("xl", "z")), own, width)


def solution(mesh):
    fine = Mesh(mesh.devices.reshape(2, -1, 2, mesh.devices.shape[1]), ("xl", "z", "c", "head"))
    spec = P(("xl", "z", "c"), "head")
    return jax.shard_map(shards, mesh=fine, in_specs=(spec,) * 5, out_specs=spec, check_vma=False)
```

```python
import functools
import math

import jax
import jax.numpy as jnp
from jax import lax
from jax.experimental import pallas as pl
from jax.experimental.pallas import tpu as pltpu
from jax.sharding import Mesh
from jax.sharding import PartitionSpec as P

HEAD = 128
LANES = 128
LOG2_SCALE = 168.0**-0.5 * math.log2(math.e)
NEG = -1e30
KEY_BLOCK = 2048
ROW_BLOCK = 256
STATS = 8
PARTS = 4

f32 = jnp.float32
bf16 = jnp.bfloat16

ATTEND_VMEM = 32 << 20
SMALL_VMEM = 4 << 20


def scores_of(a, b):
    return lax.dot_general(a, b, (((1,), (1,)), ((), ())), preferred_element_type=f32)


def split_three(value):
    high = value.astype(bf16)
    rest = value - high.astype(f32)
    middle = rest.astype(bf16)
    low = (rest - middle.astype(f32)).astype(bf16)
    return high.astype(f32), middle.astype(f32), low.astype(f32)


def packed_stats(m, l):
    pieces = (*split_three(m), *split_three(l))
    n = m.shape[0]
    row = lax.broadcasted_iota(jnp.int32, (n, STATS, LANES), 1)
    out = jnp.zeros((n, STATS, LANES), f32)
    for k, piece in enumerate(pieces):
        out = jnp.where(row == k, jnp.broadcast_to(piece[:, None, :], out.shape), out)
    return out.astype(bf16)


def unpacked_stats(stats):
    s = stats.astype(f32)
    m = (s[:, 2] + s[:, 1]) + s[:, 0]
    l = (s[:, 5] + s[:, 4]) + s[:, 3]
    return m, l


def copies_kernel(q_ref, o_ref, sems):
    copies = [pltpu.make_async_copy(q_ref, o_ref.at[n], sems.at[n]) for n in range(o_ref.shape[0])]
    for copy in copies:
        copy.start()
    for copy in copies:
        copy.wait()


def copies_of(value, n):
    return pl.pallas_call(
        copies_kernel,
        in_specs=[pl.BlockSpec(memory_space=pltpu.HBM)],
        out_specs=pl.BlockSpec(memory_space=pltpu.HBM),
        out_shape=jax.ShapeDtypeStruct((n, *value.shape), value.dtype),
        scratch_shapes=[
            pltpu.SemaphoreType.DMA((n,)),
        ],
        compiler_params=pltpu.CompilerParams(vmem_limit_bytes=SMALL_VMEM),
        name="copies",
    )(pltpu.with_memory_space_constraint(value, pltpu.HBM))


def load_kernel(k_ref, v_ref, nk_ref, nv_ref, k_out, v_out, nk_out, nv_out, sems):
    pairs = [(nk_ref, nk_out), (nv_ref, nv_out)]
    step = k_ref.shape[0] // PARTS
    for p in range(PARTS):
        span = pl.ds(p * step, step)
        pairs.append((k_ref.at[span], k_out.at[span]))
        pairs.append((v_ref.at[span, pl.ds(0, HEAD)], v_out.at[span]))
    copies = [
        pltpu.make_async_copy(source, target, sems.at[n])
        for n, (source, target) in enumerate(pairs)
    ]
    for copy in copies:
        copy.start()
    for copy in copies:
        copy.wait()


def loaded(keys, values, new_keys, new_values):
    arrays = (keys, values, new_keys, new_values)
    outs = [jax.ShapeDtypeStruct(a.shape, a.dtype) for a in arrays]
    outs[1] = jax.ShapeDtypeStruct((values.shape[0], HEAD), values.dtype)
    return pl.pallas_call(
        load_kernel,
        in_specs=[pl.BlockSpec(memory_space=pltpu.HBM)] * len(arrays),
        out_specs=[pl.BlockSpec(memory_space=pltpu.VMEM)] * len(arrays),
        out_shape=outs,
        scratch_shapes=[pltpu.SemaphoreType.DMA((2 * PARTS + 2,))],
        compiler_params=pltpu.CompilerParams(vmem_limit_bytes=SMALL_VMEM),
        cost_estimate=pl.CostEstimate(
            flops=0,
            bytes_accessed=sum(2 * a.size * a.dtype.itemsize for a in outs),
            transcendentals=0,
        ),
        name="load",
    )(*(pltpu.with_memory_space_constraint(a, pltpu.HBM) for a in arrays))


def attend_kernel(same_x, same_c, q_ref, k_ref, v0_ref, v1_ref, nk_ref, nv_ref, o_ref, *rest):
    copies = {}
    if len(rest) > 2:
        v_hbm, (v1_ref, s0, s1, sems) = v1_ref, rest
        for i in range(v_hbm.shape[0] // KEY_BLOCK):
            span = pl.ds(i * KEY_BLOCK, KEY_BLOCK)
            copies[1, i] = pltpu.make_async_copy(
                v_hbm.at[span, pl.ds(HEAD, HEAD)], v1_ref.at[span], sems.at[i]
            )
        for copy in copies.values():
            copy.start()
    else:
        s0, s1 = rest
    values = (v0_ref, v1_ref)
    tokens = q_ref.shape[0]
    own = nk_ref.shape[0]
    dests = tokens // own
    rows = 2 * tokens
    kv_heads = k_ref.shape[1] // HEAD
    blocks = k_ref.shape[0] // KEY_BLOCK
    chunks = rows // ROW_BLOCK
    x, z, c = lax.axis_index("xl"), lax.axis_index("z"), lax.axis_index("c")
    first = ((x * dests + z) * 2 + c) * own
    from_x, from_c = (x if same_x else 1 - x), (c if same_c else 1 - c)
    sb = (s0, s1)
    row = lax.broadcasted_iota(jnp.int32, (rows, LANES), 0)
    col = lax.broadcasted_iota(jnp.int32, (rows, LANES), 1)
    token = row % tokens
    position = ((from_x * dests + token // own) * 2 + from_c) * own + token % own
    seen = (col < own) & (position >= first + col)
    at = lax.broadcasted_iota(jnp.int32, (dests, own, LANES), 1)
    lane = lax.broadcasted_iota(jnp.int32, (dests, own, LANES), 2)
    ones = jnp.ones((KEY_BLOCK, LANES), bf16)
    pad = jnp.zeros((LANES - own, HEAD), bf16)
    work = [(h, i) for h in range(kv_heads) for i in range(blocks)]
    queries = [
        jnp.concatenate(
            [q_ref[:, (2 * h + g) * HEAD : (2 * h + g + 1) * HEAD] for g in range(2)], axis=0
        )
        for h in range(kv_heads)
    ]

    def score_block(n):
        h, i = work[n]
        keys = k_ref[i * KEY_BLOCK : (i + 1) * KEY_BLOCK, h * HEAD : (h + 1) * HEAD]
        sb[n % 2][...] = scores_of(queries[h], keys)

    score_block(0)
    maxima = jnp.zeros((dests, own, LANES), f32)
    sums = jnp.zeros((dests, own, LANES), f32)
    for n, (h, i) in enumerate(work):
        mine = slice(h * HEAD, (h + 1) * HEAD)
        if n + 1 < len(work):
            score_block(n + 1)
        if i == 0:
            keys = jnp.concatenate([nk_ref[:, mine], pad], axis=0)
            vals = jnp.concatenate([nv_ref[:, mine], pad], axis=0)
            s = jnp.where(seen, scores_of(queries[h], keys), NEG)
            m = jnp.broadcast_to(jnp.max(s, axis=1, keepdims=True), s.shape)
            p = jnp.where(seen, jnp.exp2((s - m) * LOG2_SCALE), 0.0).astype(bf16)
            vals = jnp.concatenate([vals, ones[:LANES]], axis=1)
            a = jnp.dot(p, vals, preferred_element_type=f32)
            acc = [a[r * ROW_BLOCK : (r + 1) * ROW_BLOCK] for r in range(chunks)]
            top = [m[r * ROW_BLOCK : (r + 1) * ROW_BLOCK] for r in range(chunks)]
        if (h, i) in copies:
            copies[h, i].wait()
        vals = jnp.concatenate([values[h][i * KEY_BLOCK : (i + 1) * KEY_BLOCK], ones], axis=1)
        for r in range(chunks):
            s = sb[n % 2][r * ROW_BLOCK : (r + 1) * ROW_BLOCK]
            m = jnp.maximum(top[r], jnp.max(s, axis=1, keepdims=True))
            p = jnp.exp2((s - jnp.tile(m, (1, KEY_BLOCK // LANES))) * LOG2_SCALE)
            decay = jnp.exp2((top[r] - m) * LOG2_SCALE)
            acc[r] = acc[r] * jnp.tile(decay, (1, 2)) + jnp.dot(
                p.astype(bf16), vals, preferred_element_type=f32
            )
            top[r] = m
        if i == blocks - 1:
            whole, whole_top = jnp.concatenate(acc, axis=0), jnp.concatenate(top, axis=0)
            for g in range(2):
                slot = h * 2 + g
                part = whole[g * tokens : (g + 1) * tokens]
                part_top = whole_top[g * tokens : (g + 1) * tokens]
                o_ref[:, slot * own : (slot + 1) * own, :] = (
                    part[:, :HEAD].reshape(dests, own, HEAD).astype(bf16)
                )
                pick = lane == slot * own + at
                maxima = maxima + jnp.where(pick, part_top.reshape(dests, own, LANES), 0.0)
                sums = sums + jnp.where(pick, part[:, HEAD:].reshape(dests, own, LANES), 0.0)
    o_ref[:, 2 * kv_heads * own :, :] = packed_stats(
        jnp.sum(maxima, axis=1), jnp.sum(sums, axis=1)
    )


def attend(same_x, same_c, queries, keys, first, second, new_keys, new_values, fetch=False):
    (tokens, width), own = queries.shape, new_keys.shape[0]
    rows, prefix = 2 * tokens, keys.shape[0]
    whole = pl.BlockSpec(memory_space=pltpu.VMEM)
    specs = [whole] * 6
    outs = [
        jax.ShapeDtypeStruct((tokens // own, width // HEAD * own + STATS, HEAD), bf16)
    ]
    scratch = [pltpu.VMEM((rows, KEY_BLOCK), f32)] * 2
    if fetch:
        specs[3] = pl.BlockSpec(memory_space=pltpu.HBM)
        outs.append(jax.ShapeDtypeStruct(first.shape, first.dtype))
        scratch.append(pltpu.SemaphoreType.DMA((prefix // KEY_BLOCK,)))
        second = pltpu.with_memory_space_constraint(second, pltpu.HBM)
    return pl.pallas_call(
        functools.partial(attend_kernel, same_x, same_c),
        in_specs=specs,
        out_specs=[whole] * len(outs),
        out_shape=outs,
        scratch_shapes=scratch,
        compiler_params=pltpu.CompilerParams(vmem_limit_bytes=ATTEND_VMEM),
        cost_estimate=pl.CostEstimate(
            flops=4 * tokens * width * prefix,
            bytes_accessed=4 * prefix * keys.shape[1],
            transcendentals=tokens * width // HEAD * prefix,
        ),
        name="attend",
    )(queries, keys, first, second, new_keys, new_values)


def columns_of(rows):
    n = rows.shape[0]
    if n < LANES:
        rows = jnp.concatenate([rows, jnp.zeros((LANES - n, LANES), f32)], axis=0)
    return jnp.transpose(rows)


def merge_kernel(here_ref, here_sib_ref, there_ref, there_sib_ref, o_ref):
    n, pairs = here_ref.shape[0], here_ref.shape[1] - STATS
    x = lax.axis_index("xl")
    for at, a_ref, b_ref in (
        (x * n, here_ref, here_sib_ref),
        ((1 - x) * n, there_ref, there_sib_ref),
    ):
        ma, la = unpacked_stats(a_ref[:, pairs:, :])
        mb, lb = unpacked_stats(b_ref[:, pairs:, :])
        m = jnp.maximum(ma, mb)
        wa, wb = jnp.exp2((ma - m) * LOG2_SCALE), jnp.exp2((mb - m) * LOG2_SCALE)
        o_ref[pl.ds(at, n), pairs:, :] = packed_stats(m, la * wa + lb * wb)
        cols = columns_of(jnp.concatenate([wa, wb], axis=0))
        for d in range(n):
            mixed = (
                a_ref[d, :pairs].astype(f32) * cols[:pairs, d : d + 1]
                + b_ref[d, :pairs].astype(f32) * cols[:pairs, n + d : n + d + 1]
            )
            o_ref[at + d, :pairs] = mixed.astype(bf16)


def merge(here, here_sib, there, there_sib):
    whole = pl.BlockSpec(memory_space=pltpu.VMEM)
    n, height, _ = here.shape
    return pl.pallas_call(
        merge_kernel,
        in_specs=[whole] * 4,
        out_specs=whole,
        out_shape=jax.ShapeDtypeStruct((2 * n, height, HEAD), bf16),
        compiler_params=pltpu.CompilerParams(vmem_limit_bytes=SMALL_VMEM),
        name="merge",
    )(here, here_sib, there, there_sib)


def finish_kernel(own, r_ref, o_ref):
    n, pairs = r_ref.shape[0], r_ref.shape[1] - STATS
    m, l = unpacked_stats(r_ref[:, pairs:, :])
    w = jnp.exp2((m - jnp.max(m, axis=0, keepdims=True)) * LOG2_SCALE)
    cols = columns_of(w / jnp.sum(l * w, axis=0, keepdims=True))
    out = r_ref[0, :pairs].astype(f32) * cols[:pairs, 0:1]
    for s in range(1, n):
        out = out + r_ref[s, :pairs].astype(f32) * cols[:pairs, s : s + 1]
    for j in range(pairs // own):
        o_ref[:, j * HEAD : (j + 1) * HEAD] = out[j * own : (j + 1) * own].astype(bf16)


def finish(received, own, width):
    whole = pl.BlockSpec(memory_space=pltpu.VMEM)
    return pl.pallas_call(
        functools.partial(finish_kernel, own),
        in_specs=[whole],
        out_specs=whole,
        out_shape=jax.ShapeDtypeStruct((own, width), bf16),
        compiler_params=pltpu.CompilerParams(vmem_limit_bytes=SMALL_VMEM),
        name="finish",
    )(received)


def exchanged(blocks, axes):
    return lax.all_to_all(blocks, axes, split_axis=0, concat_axis=0, tiled=True)


def swapped(value, axis):
    return lax.ppermute(value, axis, [(0, 1), (1, 0)])


def after(value, earlier):
    return lax.optimization_barrier((value, earlier))[0]


def shards(queries, cache_keys, prefix_cache_values, incoming_keys, incoming_values):
    own, width = queries.shape
    column = lax.axis_size("z")
    local = loaded(cache_keys, prefix_cache_values, incoming_keys, incoming_values)
    here = exchanged(copies_of(queries, column), "z")
    here, *local = lax.optimization_barrier((here, *local))
    here = here.reshape(column * own, width)
    here_other = swapped(here, "c")
    there = swapped(here, "xl")
    keys, first, *fresh = local
    part_here, second = attend(
        True, True, here, keys, first, prefix_cache_values, *fresh, fetch=True
    )
    local = (keys, first, second, *fresh)
    there, here_other, part_here = lax.optimization_barrier((there, here_other, part_here))
    there_other = swapped(there, "c")
    (part_here_other,) = attend(True, False, here_other, *local)
    here_sib = swapped(part_here_other, "c")
    (part_there_other,) = attend(False, False, after(there_other, part_here_other), *local)
    there_sib = swapped(part_there_other, "c")
    (part_there,) = attend(False, True, after(there, part_there_other), *local)
    merged = merge(part_here, here_sib, part_there, there_sib)
    return finish(exchanged(merged, ("xl", "z")), own, width)


def solution(mesh):
    fine = Mesh(mesh.devices.reshape(2, -1, 2, mesh.devices.shape[1]), ("xl", "z", "c", "head"))
    spec = P(("xl", "z", "c"), "head")
    return jax.shard_map(shards, mesh=fine, in_specs=(spec,) * 5, out_specs=spec, check_vma=False)
```

```python
import functools
import math

import jax
import jax.numpy as jnp
from jax import lax
from jax.experimental import pallas as pl
from jax.experimental.pallas import tpu as pltpu
from jax.sharding import Mesh
from jax.sharding import PartitionSpec as P

HEAD = 128
LANES = 128
LOG2_SCALE = 168.0**-0.5 * math.log2(math.e)
NEG = -1e30
KEY_BLOCK = 2048
ROW_BLOCK = 256
STATS = 8
PARTS = 4

Z_ORDER = (7, 3, 6, 2, 5, 1, 4, 0)
RETURN_ORDER = tuple((x if z % 2 else 1 - x, z) for z in range(7, -1, -1) for x in range(2))

f32 = jnp.float32
bf16 = jnp.bfloat16

ATTEND_VMEM = 32 << 20
SMALL_VMEM = 4 << 20


def scores_of(a, b):
    return lax.dot_general(a, b, (((1,), (1,)), ((), ())), preferred_element_type=f32)


def split_three(value):
    high = value.astype(bf16)
    rest = value - high.astype(f32)
    middle = rest.astype(bf16)
    low = (rest - middle.astype(f32)).astype(bf16)
    return high.astype(f32), middle.astype(f32), low.astype(f32)


def packed_stats(m, l):
    pieces = (*split_three(m), *split_three(l))
    n = m.shape[0]
    row = lax.broadcasted_iota(jnp.int32, (n, STATS, LANES), 1)
    out = jnp.zeros((n, STATS, LANES), f32)
    for k, piece in enumerate(pieces):
        out = jnp.where(row == k, jnp.broadcast_to(piece[:, None, :], out.shape), out)
    return out.astype(bf16)


def unpacked_stats(stats):
    s = stats.astype(f32)
    m = (s[:, 2] + s[:, 1]) + s[:, 0]
    l = (s[:, 5] + s[:, 4]) + s[:, 3]
    return m, l


def load_kernel(k_ref, v_ref, nk_ref, nv_ref, k_out, v_out, nk_out, nv_out, sems):
    pairs = [(nk_ref, nk_out), (nv_ref, nv_out)]
    step = k_ref.shape[0] // PARTS
    for p in range(PARTS):
        span = pl.ds(p * step, step)
        pairs.append((k_ref.at[span], k_out.at[span]))
        pairs.append((v_ref.at[span, pl.ds(0, HEAD)], v_out.at[span]))
    copies = [
        pltpu.make_async_copy(source, target, sems.at[n])
        for n, (source, target) in enumerate(pairs)
    ]
    for copy in copies:
        copy.start()
    for copy in copies:
        copy.wait()


def loaded(keys, values, new_keys, new_values):
    arrays = (keys, values, new_keys, new_values)
    outs = [jax.ShapeDtypeStruct(a.shape, a.dtype) for a in arrays]
    outs[1] = jax.ShapeDtypeStruct((values.shape[0], HEAD), values.dtype)
    return pl.pallas_call(
        load_kernel,
        in_specs=[pl.BlockSpec(memory_space=pltpu.HBM)] * len(arrays),
        out_specs=[pl.BlockSpec(memory_space=pltpu.VMEM)] * len(arrays),
        out_shape=outs,
        scratch_shapes=[pltpu.SemaphoreType.DMA((2 * PARTS + 2,))],
        compiler_params=pltpu.CompilerParams(vmem_limit_bytes=SMALL_VMEM),
        cost_estimate=pl.CostEstimate(
            flops=0,
            bytes_accessed=sum(2 * a.size * a.dtype.itemsize for a in outs),
            transcendentals=0,
        ),
        name="load",
    )(*(pltpu.with_memory_space_constraint(a, pltpu.HBM) for a in arrays))


def attend_kernel(same_x, same_c, q_ref, k_ref, v0_ref, v1_ref, nk_ref, nv_ref, o_ref, *rest):
    copies = {}
    if len(rest) > 2:
        v_hbm, (v1_ref, s0, s1, sems) = v1_ref, rest
        for i in range(v_hbm.shape[0] // KEY_BLOCK):
            span = pl.ds(i * KEY_BLOCK, KEY_BLOCK)
            copies[1, i] = pltpu.make_async_copy(
                v_hbm.at[span, pl.ds(HEAD, HEAD)], v1_ref.at[span], sems.at[i]
            )
        for copy in copies.values():
            copy.start()
    else:
        s0, s1 = rest
    values = (v0_ref, v1_ref)
    tokens = q_ref.shape[0]
    own = nk_ref.shape[0]
    dests = tokens // own
    rows = 2 * tokens
    kv_heads = k_ref.shape[1] // HEAD
    blocks = k_ref.shape[0] // KEY_BLOCK
    chunks = rows // ROW_BLOCK
    x, z, c = lax.axis_index("xl"), lax.axis_index("z"), lax.axis_index("c")
    first = ((x * dests + z) * 2 + c) * own
    from_x, from_c = (x if same_x else 1 - x), (c if same_c else 1 - c)
    sb = (s0, s1)
    col = lax.broadcasted_iota(jnp.int32, (rows, LANES), 1)
    within = lax.broadcasted_iota(jnp.int32, (own, LANES), 0)
    position = jnp.concatenate(
        [((from_x * dests + z_from) * 2 + from_c) * own + within for z_from in Z_ORDER] * 2, axis=0
    )
    seen = (col < own) & (position >= first + col)
    at = lax.broadcasted_iota(jnp.int32, (dests, own, LANES), 1)
    lane = lax.broadcasted_iota(jnp.int32, (dests, own, LANES), 2)
    ones = jnp.ones((KEY_BLOCK, LANES), bf16)
    pad = jnp.zeros((LANES - own, HEAD), bf16)
    work = [(h, i) for h in range(kv_heads) for i in range(blocks)]
    queries = [
        jnp.concatenate(
            [q_ref[:, (2 * h + g) * HEAD : (2 * h + g + 1) * HEAD] for g in range(2)], axis=0
        )
        for h in range(kv_heads)
    ]

    def score_block(n):
        h, i = work[n]
        keys = k_ref[i * KEY_BLOCK : (i + 1) * KEY_BLOCK, h * HEAD : (h + 1) * HEAD]
        sb[n % 2][...] = scores_of(queries[h], keys)

    score_block(0)
    maxima = jnp.zeros((dests, own, LANES), f32)
    sums = jnp.zeros((dests, own, LANES), f32)
    for n, (h, i) in enumerate(work):
        mine = slice(h * HEAD, (h + 1) * HEAD)
        if n + 1 < len(work):
            score_block(n + 1)
        if i == 0:
            keys = jnp.concatenate([nk_ref[:, mine], pad], axis=0)
            vals = jnp.concatenate([nv_ref[:, mine], pad], axis=0)
            s = jnp.where(seen, scores_of(queries[h], keys), NEG)
            m = jnp.broadcast_to(jnp.max(s, axis=1, keepdims=True), s.shape)
            p = jnp.where(seen, jnp.exp2((s - m) * LOG2_SCALE), 0.0).astype(bf16)
            vals = jnp.concatenate([vals, ones[:LANES]], axis=1)
            a = jnp.dot(p, vals, preferred_element_type=f32)
            acc = [a[r * ROW_BLOCK : (r + 1) * ROW_BLOCK] for r in range(chunks)]
            top = [m[r * ROW_BLOCK : (r + 1) * ROW_BLOCK] for r in range(chunks)]
        if (h, i) in copies:
            copies[h, i].wait()
        vals = jnp.concatenate([values[h][i * KEY_BLOCK : (i + 1) * KEY_BLOCK], ones], axis=1)
        for r in range(chunks):
            s = sb[n % 2][r * ROW_BLOCK : (r + 1) * ROW_BLOCK]
            m = jnp.maximum(top[r], jnp.max(s, axis=1, keepdims=True))
            p = jnp.exp2((s - jnp.tile(m, (1, KEY_BLOCK // LANES))) * LOG2_SCALE)
            decay = jnp.exp2((top[r] - m) * LOG2_SCALE)
            acc[r] = acc[r] * jnp.tile(decay, (1, 2)) + jnp.dot(
                p.astype(bf16), vals, preferred_element_type=f32
            )
            top[r] = m
        if i == blocks - 1:
            whole, whole_top = jnp.concatenate(acc, axis=0), jnp.concatenate(top, axis=0)
            for g in range(2):
                slot = h * 2 + g
                part = whole[g * tokens : (g + 1) * tokens]
                part_top = whole_top[g * tokens : (g + 1) * tokens]
                o_ref[:, slot * own : (slot + 1) * own, :] = (
                    part[:, :HEAD].reshape(dests, own, HEAD).astype(bf16)
                )
                pick = lane == slot * own + at
                maxima = maxima + jnp.where(pick, part_top.reshape(dests, own, LANES), 0.0)
                sums = sums + jnp.where(pick, part[:, HEAD:].reshape(dests, own, LANES), 0.0)
    o_ref[:, 2 * kv_heads * own :, :] = packed_stats(
        jnp.sum(maxima, axis=1), jnp.sum(sums, axis=1)
    )


def attend(same_x, same_c, queries, keys, first, second, new_keys, new_values, fetch=False):
    (tokens, width), own = queries.shape, new_keys.shape[0]
    rows, prefix = 2 * tokens, keys.shape[0]
    whole = pl.BlockSpec(memory_space=pltpu.VMEM)
    specs = [whole] * 6
    outs = [
        jax.ShapeDtypeStruct((tokens // own, width // HEAD * own + STATS, HEAD), bf16)
    ]
    scratch = [pltpu.VMEM((rows, KEY_BLOCK), f32)] * 2
    if fetch:
        specs[3] = pl.BlockSpec(memory_space=pltpu.HBM)
        outs.append(jax.ShapeDtypeStruct(first.shape, first.dtype))
        scratch.append(pltpu.SemaphoreType.DMA((prefix // KEY_BLOCK,)))
        second = pltpu.with_memory_space_constraint(second, pltpu.HBM)
    return pl.pallas_call(
        functools.partial(attend_kernel, same_x, same_c),
        in_specs=specs,
        out_specs=[whole] * len(outs),
        out_shape=outs,
        scratch_shapes=scratch,
        compiler_params=pltpu.CompilerParams(vmem_limit_bytes=ATTEND_VMEM),
        cost_estimate=pl.CostEstimate(
            flops=4 * tokens * width * prefix,
            bytes_accessed=4 * prefix * keys.shape[1],
            transcendentals=tokens * width // HEAD * prefix,
        ),
        name="attend",
    )(queries, keys, first, second, new_keys, new_values)


def columns_of(rows):
    n = rows.shape[0]
    if n < LANES:
        rows = jnp.concatenate([rows, jnp.zeros((LANES - n, LANES), f32)], axis=0)
    return jnp.transpose(rows)


def merge_kernel(here_ref, here_sib_ref, there_ref, there_sib_ref, o_ref):
    n, pairs = here_ref.shape[0], here_ref.shape[1] - STATS
    x = lax.axis_index("xl")
    for column, a_ref, b_ref in (
        (x, here_ref, here_sib_ref),
        (1 - x, there_ref, there_sib_ref),
    ):
        ma, la = unpacked_stats(a_ref[:, pairs:, :])
        mb, lb = unpacked_stats(b_ref[:, pairs:, :])
        m = jnp.maximum(ma, mb)
        wa, wb = jnp.exp2((ma - m) * LOG2_SCALE), jnp.exp2((mb - m) * LOG2_SCALE)
        stats = packed_stats(m, la * wa + lb * wb)
        cols = columns_of(jnp.concatenate([wa, wb], axis=0))
        for d in range(n):
            slots = [RETURN_ORDER.index((k, Z_ORDER[d])) for k in range(2)]
            slot = jnp.where(column == 0, slots[0], slots[1])
            mixed = (
                a_ref[d, :pairs].astype(f32) * cols[:pairs, d : d + 1]
                + b_ref[d, :pairs].astype(f32) * cols[:pairs, n + d : n + d + 1]
            )
            o_ref[slot, :pairs] = mixed.astype(bf16)
            o_ref[slot, pairs:] = stats[d]


def merge(here, here_sib, there, there_sib):
    whole = pl.BlockSpec(memory_space=pltpu.VMEM)
    n, height, _ = here.shape
    return pl.pallas_call(
        merge_kernel,
        in_specs=[whole] * 4,
        out_specs=whole,
        out_shape=jax.ShapeDtypeStruct((2 * n, height, HEAD), bf16),
        compiler_params=pltpu.CompilerParams(vmem_limit_bytes=SMALL_VMEM),
        name="merge",
    )(here, here_sib, there, there_sib)


def finish_kernel(own, r_ref, o_ref):
    n, pairs = r_ref.shape[0], r_ref.shape[1] - STATS
    m, l = unpacked_stats(r_ref[:, pairs:, :])
    w = jnp.exp2((m - jnp.max(m, axis=0, keepdims=True)) * LOG2_SCALE)
    cols = columns_of(w / jnp.sum(l * w, axis=0, keepdims=True))
    out = r_ref[0, :pairs].astype(f32) * cols[:pairs, 0:1]
    for s in range(1, n):
        out = out + r_ref[s, :pairs].astype(f32) * cols[:pairs, s : s + 1]
    for j in range(pairs // own):
        o_ref[:, j * HEAD : (j + 1) * HEAD] = out[j * own : (j + 1) * own].astype(bf16)


def finish(received, own, width):
    whole = pl.BlockSpec(memory_space=pltpu.VMEM)
    return pl.pallas_call(
        functools.partial(finish_kernel, own),
        in_specs=[whole],
        out_specs=whole,
        out_shape=jax.ShapeDtypeStruct((own, width), bf16),
        compiler_params=pltpu.CompilerParams(vmem_limit_bytes=SMALL_VMEM),
        name="finish",
    )(received)


def exchanged(blocks, axes, order):
    return lax.all_to_all(
        blocks, axes, split_axis=0, concat_axis=0, tiled=True, axis_index_groups=[list(order)]
    )


def swapped(value, axis):
    return lax.ppermute(value, axis, [(0, 1), (1, 0)])


def after(value, earlier):
    return lax.optimization_barrier((value, earlier))[0]


def shards(queries, cache_keys, prefix_cache_values, incoming_keys, incoming_values):
    own, width = queries.shape
    column = lax.axis_size("z")
    local = loaded(cache_keys, prefix_cache_values, incoming_keys, incoming_values)
    here = exchanged(jnp.broadcast_to(queries, (column, own, width)), "z", Z_ORDER)
    here, *local = lax.optimization_barrier((here, *local))
    here = here.reshape(column * own, width)
    here_other = swapped(here, "c")
    there = swapped(here, "xl")
    keys, first, *fresh = local
    part_here, second = attend(
        True, True, here, keys, first, prefix_cache_values, *fresh, fetch=True
    )
    local = (keys, first, second, *fresh)
    there, here_other, part_here = lax.optimization_barrier((there, here_other, part_here))
    there_other = swapped(there, "c")
    (part_here_other,) = attend(True, False, here_other, *local)
    here_sib = swapped(part_here_other, "c")
    (part_there_other,) = attend(False, False, after(there_other, part_here_other), *local)
    there_sib = swapped(part_there_other, "c")
    (part_there,) = attend(False, True, after(there, part_there_other), *local)
    merged = merge(part_here, here_sib, part_there, there_sib)
    back = [x * column + z for x, z in RETURN_ORDER]
    return finish(exchanged(merged, ("xl", "z"), back), own, width)


def solution(mesh):
    fine = Mesh(mesh.devices.reshape(2, -1, 2, mesh.devices.shape[1]), ("xl", "z", "c", "head"))
    spec = P(("xl", "z", "c"), "head")
    return jax.shard_map(shards, mesh=fine, in_specs=(spec,) * 5, out_specs=spec, check_vma=False)
```

```python
import functools
import math

import jax
import jax.numpy as jnp
from jax import lax
from jax.experimental import pallas as pl
from jax.experimental.pallas import tpu as pltpu
from jax.sharding import Mesh
from jax.sharding import PartitionSpec as P

HEAD = 128
LANES = 128
LOG2_SCALE = 168.0**-0.5 * math.log2(math.e)
NEG = -1e30
KEY_BLOCK = 2048
ROW_BLOCK = 256
STATS = 8
PARTS = 4

Z_ORDER = (7, 3, 6, 2, 5, 1, 4, 0)
RETURN_ORDER = tuple((x if z % 2 else 1 - x, z) for z in range(7, -1, -1) for x in range(2))

f32 = jnp.float32
bf16 = jnp.bfloat16

ATTEND_VMEM = 32 << 20
SMALL_VMEM = 4 << 20


def scores_of(a, b):
    return lax.dot_general(a, b, (((1,), (1,)), ((), ())), preferred_element_type=f32)


def split_three(value):
    high = value.astype(bf16)
    rest = value - high.astype(f32)
    middle = rest.astype(bf16)
    low = (rest - middle.astype(f32)).astype(bf16)
    return high.astype(f32), middle.astype(f32), low.astype(f32)


def packed_stats(m, l):
    pieces = (*split_three(m), *split_three(l))
    n = m.shape[0]
    row = lax.broadcasted_iota(jnp.int32, (n, STATS, LANES), 1)
    out = jnp.zeros((n, STATS, LANES), f32)
    for k, piece in enumerate(pieces):
        out = jnp.where(row == k, jnp.broadcast_to(piece[:, None, :], out.shape), out)
    return out.astype(bf16)


def unpacked_stats(stats):
    s = stats.astype(f32)
    m = (s[:, 2] + s[:, 1]) + s[:, 0]
    l = (s[:, 5] + s[:, 4]) + s[:, 3]
    return m, l


def load_kernel(k_ref, v_ref, nk_ref, nv_ref, k_out, v_out, nk_out, nv_out, sems):
    pairs = [(nk_ref, nk_out), (nv_ref, nv_out)]
    step = k_ref.shape[0] // PARTS
    for p in range(PARTS):
        span = pl.ds(p * step, step)
        pairs.append((k_ref.at[span], k_out.at[span]))
        pairs.append((v_ref.at[span, pl.ds(0, HEAD)], v_out.at[span]))
    copies = [
        pltpu.make_async_copy(source, target, sems.at[n])
        for n, (source, target) in enumerate(pairs)
    ]
    for copy in copies:
        copy.start()
    for copy in copies:
        copy.wait()


def loaded(keys, values, new_keys, new_values):
    arrays = (keys, values, new_keys, new_values)
    outs = [jax.ShapeDtypeStruct(a.shape, a.dtype) for a in arrays]
    outs[1] = jax.ShapeDtypeStruct((values.shape[0], HEAD), values.dtype)
    return pl.pallas_call(
        load_kernel,
        in_specs=[pl.BlockSpec(memory_space=pltpu.HBM)] * len(arrays),
        out_specs=[pl.BlockSpec(memory_space=pltpu.VMEM)] * len(arrays),
        out_shape=outs,
        scratch_shapes=[pltpu.SemaphoreType.DMA((2 * PARTS + 2,))],
        compiler_params=pltpu.CompilerParams(vmem_limit_bytes=SMALL_VMEM),
        cost_estimate=pl.CostEstimate(
            flops=0,
            bytes_accessed=sum(2 * a.size * a.dtype.itemsize for a in outs),
            transcendentals=0,
        ),
        name="load",
    )(*(pltpu.with_memory_space_constraint(a, pltpu.HBM) for a in arrays))


def attend_kernel(same_x, same_c, q_ref, k_ref, v0_ref, v1_ref, nk_ref, nv_ref, o_ref, *rest):
    copies = {}
    if len(rest) > 2:
        v_hbm, (v1_ref, s0, s1, sems) = v1_ref, rest
        copies[1] = pltpu.make_async_copy(v_hbm.at[:, pl.ds(HEAD, HEAD)], v1_ref, sems.at[0])
        copies[1].start()
    else:
        s0, s1 = rest
    values = (v0_ref, v1_ref)
    tokens = q_ref.shape[0]
    own = nk_ref.shape[0]
    dests = tokens // own
    rows = 2 * tokens
    kv_heads = k_ref.shape[1] // HEAD
    chunks = rows // ROW_BLOCK
    x, z, c = lax.axis_index("xl"), lax.axis_index("z"), lax.axis_index("c")
    first = ((x * dests + z) * 2 + c) * own
    from_x, from_c = (x if same_x else 1 - x), (c if same_c else 1 - c)
    sb = (s0, s1)
    col = lax.broadcasted_iota(jnp.int32, (rows, LANES), 1)
    within = lax.broadcasted_iota(jnp.int32, (own, LANES), 0)
    position = jnp.concatenate(
        [((from_x * dests + z_from) * 2 + from_c) * own + within for z_from in Z_ORDER] * 2, axis=0
    )
    seen = (col < own) & (position >= first + col)
    at = lax.broadcasted_iota(jnp.int32, (dests, own, LANES), 1)
    lane = lax.broadcasted_iota(jnp.int32, (dests, own, LANES), 2)
    ones = jnp.ones((KEY_BLOCK, LANES), bf16)
    pad = jnp.zeros((LANES - own, HEAD), bf16)
    work = [
        (h, slice(start, start + KEY_BLOCK))
        for h in range(kv_heads)
        for start in range(0, k_ref.shape[0], KEY_BLOCK)
    ]
    queries = [
        jnp.concatenate(
            [q_ref[:, (2 * h + g) * HEAD : (2 * h + g + 1) * HEAD] for g in range(2)], axis=0
        )
        for h in range(kv_heads)
    ]

    def score_block(n):
        h, span = work[n]
        keys = k_ref[span, h * HEAD : (h + 1) * HEAD]
        sb[n % 2][...] = scores_of(queries[h], keys)

    score_block(0)
    maxima = jnp.zeros((dests, own, LANES), f32)
    sums = jnp.zeros((dests, own, LANES), f32)
    for n, (h, span) in enumerate(work):
        mine = slice(h * HEAD, (h + 1) * HEAD)
        if n + 1 < len(work):
            score_block(n + 1)
        if span.start == 0:
            keys = jnp.concatenate([nk_ref[:, mine], pad], axis=0)
            vals = jnp.concatenate([nv_ref[:, mine], pad], axis=0)
            s = jnp.where(seen, scores_of(queries[h], keys), NEG)
            m = jnp.broadcast_to(jnp.max(s, axis=1, keepdims=True), s.shape)
            p = jnp.where(seen, jnp.exp2((s - m) * LOG2_SCALE), 0.0).astype(bf16)
            vals = jnp.concatenate([vals, ones[:LANES]], axis=1)
            a = jnp.dot(p, vals, preferred_element_type=f32)
            acc = [a[r * ROW_BLOCK : (r + 1) * ROW_BLOCK] for r in range(chunks)]
            top = [m[r * ROW_BLOCK : (r + 1) * ROW_BLOCK] for r in range(chunks)]
        if h in copies:
            copies.pop(h).wait()
        vals = jnp.concatenate([values[h][span], ones], axis=1)
        for r in range(chunks):
            s = sb[n % 2][r * ROW_BLOCK : (r + 1) * ROW_BLOCK]
            m = jnp.maximum(top[r], jnp.max(s, axis=1, keepdims=True))
            p = jnp.exp2((s - jnp.tile(m, (1, KEY_BLOCK // LANES))) * LOG2_SCALE)
            decay = jnp.exp2((top[r] - m) * LOG2_SCALE)
            acc[r] = acc[r] * jnp.tile(decay, (1, 2)) + jnp.dot(
                p.astype(bf16), vals, preferred_element_type=f32
            )
            top[r] = m
        if span.stop == k_ref.shape[0]:
            whole, whole_top = jnp.concatenate(acc, axis=0), jnp.concatenate(top, axis=0)
            for g in range(2):
                slot = h * 2 + g
                part = whole[g * tokens : (g + 1) * tokens]
                part_top = whole_top[g * tokens : (g + 1) * tokens]
                o_ref[:, slot * own : (slot + 1) * own, :] = (
                    part[:, :HEAD].reshape(dests, own, HEAD).astype(bf16)
                )
                pick = lane == slot * own + at
                maxima = maxima + jnp.where(pick, part_top.reshape(dests, own, LANES), 0.0)
                sums = sums + jnp.where(pick, part[:, HEAD:].reshape(dests, own, LANES), 0.0)
    o_ref[:, 2 * kv_heads * own :, :] = packed_stats(
        jnp.sum(maxima, axis=1), jnp.sum(sums, axis=1)
    )


def attend(same_x, same_c, queries, keys, first, second, new_keys, new_values, fetch=False):
    (tokens, width), own = queries.shape, new_keys.shape[0]
    rows, prefix = 2 * tokens, keys.shape[0]
    whole = pl.BlockSpec(memory_space=pltpu.VMEM)
    specs = [whole] * 6
    outs = [
        jax.ShapeDtypeStruct((tokens // own, width // HEAD * own + STATS, HEAD), bf16)
    ]
    scratch = [pltpu.VMEM((rows, KEY_BLOCK), f32)] * 2
    if fetch:
        specs[3] = pl.BlockSpec(memory_space=pltpu.HBM)
        outs.append(jax.ShapeDtypeStruct(first.shape, first.dtype))
        scratch.append(pltpu.SemaphoreType.DMA((1,)))
        second = pltpu.with_memory_space_constraint(second, pltpu.HBM)
    return pl.pallas_call(
        functools.partial(attend_kernel, same_x, same_c),
        in_specs=specs,
        out_specs=[whole] * len(outs),
        out_shape=outs,
        scratch_shapes=scratch,
        compiler_params=pltpu.CompilerParams(vmem_limit_bytes=ATTEND_VMEM),
        cost_estimate=pl.CostEstimate(
            flops=4 * tokens * width * prefix,
            bytes_accessed=4 * prefix * keys.shape[1],
            transcendentals=tokens * width // HEAD * prefix,
        ),
        name="attend",
    )(queries, keys, first, second, new_keys, new_values)


def columns_of(rows):
    n = rows.shape[0]
    if n < LANES:
        rows = jnp.concatenate([rows, jnp.zeros((LANES - n, LANES), f32)], axis=0)
    return jnp.transpose(rows)


def merge_kernel(here_ref, here_sib_ref, there_ref, there_sib_ref, o_ref):
    n, pairs = here_ref.shape[0], here_ref.shape[1] - STATS
    x = lax.axis_index("xl")
    for column, a_ref, b_ref in (
        (x, here_ref, here_sib_ref),
        (1 - x, there_ref, there_sib_ref),
    ):
        ma, la = unpacked_stats(a_ref[:, pairs:, :])
        mb, lb = unpacked_stats(b_ref[:, pairs:, :])
        m = jnp.maximum(ma, mb)
        wa, wb = jnp.exp2((ma - m) * LOG2_SCALE), jnp.exp2((mb - m) * LOG2_SCALE)
        stats = packed_stats(m, la * wa + lb * wb)
        cols = columns_of(jnp.concatenate([wa, wb], axis=0))
        for d in range(n):
            slots = [RETURN_ORDER.index((k, Z_ORDER[d])) for k in range(2)]
            slot = jnp.where(column == 0, slots[0], slots[1])
            mixed = (
                a_ref[d, :pairs].astype(f32) * cols[:pairs, d : d + 1]
                + b_ref[d, :pairs].astype(f32) * cols[:pairs, n + d : n + d + 1]
            )
            o_ref[slot, :pairs] = mixed.astype(bf16)
            o_ref[slot, pairs:] = stats[d]


def merge(here, here_sib, there, there_sib):
    whole = pl.BlockSpec(memory_space=pltpu.VMEM)
    n, height, _ = here.shape
    return pl.pallas_call(
        merge_kernel,
        in_specs=[whole] * 4,
        out_specs=whole,
        out_shape=jax.ShapeDtypeStruct((2 * n, height, HEAD), bf16),
        compiler_params=pltpu.CompilerParams(vmem_limit_bytes=SMALL_VMEM),
        name="merge",
    )(here, here_sib, there, there_sib)


def finish_kernel(own, r_ref, o_ref):
    n, pairs = r_ref.shape[0], r_ref.shape[1] - STATS
    m, l = unpacked_stats(r_ref[:, pairs:, :])
    w = jnp.exp2((m - jnp.max(m, axis=0, keepdims=True)) * LOG2_SCALE)
    cols = columns_of(w / jnp.sum(l * w, axis=0, keepdims=True))
    out = r_ref[0, :pairs].astype(f32) * cols[:pairs, 0:1]
    for s in range(1, n):
        out = out + r_ref[s, :pairs].astype(f32) * cols[:pairs, s : s + 1]
    for j in range(pairs // own):
        o_ref[:, j * HEAD : (j + 1) * HEAD] = out[j * own : (j + 1) * own].astype(bf16)


def finish(received, own, width):
    whole = pl.BlockSpec(memory_space=pltpu.VMEM)
    return pl.pallas_call(
        functools.partial(finish_kernel, own),
        in_specs=[whole],
        out_specs=whole,
        out_shape=jax.ShapeDtypeStruct((own, width), bf16),
        compiler_params=pltpu.CompilerParams(vmem_limit_bytes=SMALL_VMEM),
        name="finish",
    )(received)


def exchanged(blocks, axes, order):
    return lax.all_to_all(
        blocks, axes, split_axis=0, concat_axis=0, tiled=True, axis_index_groups=[list(order)]
    )


def swapped(value, axis):
    return lax.ppermute(value, axis, [(0, 1), (1, 0)])


def after(value, earlier):
    return lax.optimization_barrier((value, earlier))[0]


def shards(queries, cache_keys, prefix_cache_values, incoming_keys, incoming_values):
    own, width = queries.shape
    column = lax.axis_size("z")
    local = loaded(cache_keys, prefix_cache_values, incoming_keys, incoming_values)
    here = exchanged(jnp.broadcast_to(queries, (column, own, width)), "z", Z_ORDER)
    here, *local = lax.optimization_barrier((here, *local))
    here = here.reshape(column * own, width)
    here_other = swapped(here, "c")
    there_other = lax.ppermute(here, ("xl", "c"), [(n, 3 - n) for n in range(4)])
    keys, first, *fresh = local
    part_here, second = attend(
        True, True, here, keys, first, prefix_cache_values, *fresh, fetch=True
    )
    local = (keys, first, second, *fresh)
    here, here_other, part_here = lax.optimization_barrier((here, here_other, part_here))
    there = swapped(here, "xl")
    (part_here_other,) = attend(True, False, here_other, *local)
    here_sib = swapped(part_here_other, "c")
    (part_there_other,) = attend(False, False, after(there_other, part_here_other), *local)
    there_sib = swapped(part_there_other, "c")
    (part_there,) = attend(False, True, after(there, part_there_other), *local)
    merged = merge(part_here, here_sib, part_there, there_sib)
    back = [x * column + z for x, z in RETURN_ORDER]
    return finish(exchanged(merged, ("xl", "z"), back), own, width)


def solution(mesh):
    fine = Mesh(mesh.devices.reshape(2, -1, 2, mesh.devices.shape[1]), ("xl", "z", "c", "head"))
    spec = P(("xl", "z", "c"), "head")
    return jax.shard_map(shards, mesh=fine, in_specs=(spec,) * 5, out_specs=spec, check_vma=False)
```

```python
import functools
import math

import jax
import jax.numpy as jnp
from jax import lax
from jax.experimental import pallas as pl
from jax.experimental.pallas import tpu as pltpu
from jax.sharding import Mesh
from jax.sharding import PartitionSpec as P

HEAD = 128
LANES = 128
LOG2_SCALE = 168.0**-0.5 * math.log2(math.e)
NEG = -1e30
KEY_BLOCK = 2048
ROW_BLOCK = 256
STATS = 8
PARTS = 4

Z_ORDER = (7, 3, 6, 2, 5, 1, 4, 0)
RETURN_ORDER = tuple((x if z % 2 else 1 - x, z) for z in range(7, -1, -1) for x in range(2))

f32 = jnp.float32
bf16 = jnp.bfloat16

ATTEND_VMEM = 32 << 20
SMALL_VMEM = 4 << 20


def scores_of(a, b):
    return lax.dot_general(a, b, (((1,), (1,)), ((), ())), preferred_element_type=f32)


def split_three(value):
    high = value.astype(bf16)
    rest = value - high.astype(f32)
    middle = rest.astype(bf16)
    low = (rest - middle.astype(f32)).astype(bf16)
    return high.astype(f32), middle.astype(f32), low.astype(f32)


def packed_stats(m, l):
    pieces = (*split_three(m), *split_three(l))
    n = m.shape[0]
    row = lax.broadcasted_iota(jnp.int32, (n, STATS, LANES), 1)
    out = jnp.zeros((n, STATS, LANES), f32)
    for k, piece in enumerate(pieces):
        out = jnp.where(row == k, jnp.broadcast_to(piece[:, None, :], out.shape), out)
    return out.astype(bf16)


def unpacked_stats(stats):
    s = stats.astype(f32)
    m = (s[:, 2] + s[:, 1]) + s[:, 0]
    l = (s[:, 5] + s[:, 4]) + s[:, 3]
    return m, l


def load_kernel(k_ref, v_ref, nk_ref, nv_ref, k_out, v_out, nk_out, nv_out, sems):
    pairs = [(nk_ref, nk_out), (nv_ref, nv_out)]
    step = k_ref.shape[0] // PARTS
    for p in range(PARTS):
        span = pl.ds(p * step, step)
        pairs.append((k_ref.at[span], k_out.at[span]))
        pairs.append((v_ref.at[span, pl.ds(0, HEAD)], v_out.at[span]))
    copies = [
        pltpu.make_async_copy(source, target, sems.at[n])
        for n, (source, target) in enumerate(pairs)
    ]
    for copy in copies:
        copy.start()
    for copy in copies:
        copy.wait()


def loaded(keys, values, new_keys, new_values):
    arrays = (keys, values, new_keys, new_values)
    outs = [jax.ShapeDtypeStruct(a.shape, a.dtype) for a in arrays]
    outs[1] = jax.ShapeDtypeStruct((values.shape[0], HEAD), values.dtype)
    return pl.pallas_call(
        load_kernel,
        in_specs=[pl.BlockSpec(memory_space=pltpu.HBM)] * len(arrays),
        out_specs=[pl.BlockSpec(memory_space=pltpu.VMEM)] * len(arrays),
        out_shape=outs,
        scratch_shapes=[pltpu.SemaphoreType.DMA((2 * PARTS + 2,))],
        compiler_params=pltpu.CompilerParams(vmem_limit_bytes=SMALL_VMEM),
        cost_estimate=pl.CostEstimate(
            flops=0,
            bytes_accessed=sum(2 * a.size * a.dtype.itemsize for a in outs),
            transcendentals=0,
        ),
        name="load",
    )(*(pltpu.with_memory_space_constraint(a, pltpu.HBM) for a in arrays))


def attend_kernel(same_x, same_c, q_ref, k_ref, v0_ref, v1_ref, nk_ref, nv_ref, o_ref, *rest):
    copies = {}
    if len(rest) == 3:
        carried_ref, s0, s1 = (o_ref, *rest[1:])
        o_ref = rest[0]
        o_ref[o_ref.shape[0] // 2 :] = carried_ref[...]
    elif len(rest) > 2:
        v_hbm, (v1_ref, s0, s1, sems) = v1_ref, rest
        copies[1] = pltpu.make_async_copy(v_hbm.at[:, pl.ds(HEAD, HEAD)], v1_ref, sems.at[0])
        copies[1].start()
    else:
        s0, s1 = rest
    values = (v0_ref, v1_ref)
    tokens = q_ref.shape[0]
    own = nk_ref.shape[0]
    dests = tokens // own
    rows = 2 * tokens
    kv_heads = k_ref.shape[1] // HEAD
    chunks = rows // ROW_BLOCK
    x, z, c = lax.axis_index("xl"), lax.axis_index("z"), lax.axis_index("c")
    first = ((x * dests + z) * 2 + c) * own
    from_x, from_c = (x if same_x else 1 - x), (c if same_c else 1 - c)
    sb = (s0, s1)
    col = lax.broadcasted_iota(jnp.int32, (rows, LANES), 1)
    within = lax.broadcasted_iota(jnp.int32, (own, LANES), 0)
    position = jnp.concatenate(
        [((from_x * dests + z_from) * 2 + from_c) * own + within for z_from in Z_ORDER] * 2, axis=0
    )
    seen = (col < own) & (position >= first + col)
    at = lax.broadcasted_iota(jnp.int32, (dests, own, LANES), 1)
    lane = lax.broadcasted_iota(jnp.int32, (dests, own, LANES), 2)
    ones = jnp.ones((KEY_BLOCK, LANES), bf16)
    pad = jnp.zeros((LANES - own, HEAD), bf16)
    work = [
        (h, slice(start, start + KEY_BLOCK))
        for h in range(kv_heads)
        for start in range(0, k_ref.shape[0], KEY_BLOCK)
    ]
    queries = [
        jnp.concatenate(
            [q_ref[:, (2 * h + g) * HEAD : (2 * h + g + 1) * HEAD] for g in range(2)], axis=0
        )
        for h in range(kv_heads)
    ]

    def score_block(n):
        h, span = work[n]
        keys = k_ref[span, h * HEAD : (h + 1) * HEAD]
        sb[n % 2][...] = scores_of(queries[h], keys)

    score_block(0)
    maxima = jnp.zeros((dests, own, LANES), f32)
    sums = jnp.zeros((dests, own, LANES), f32)
    for n, (h, span) in enumerate(work):
        mine = slice(h * HEAD, (h + 1) * HEAD)
        if n + 1 < len(work):
            score_block(n + 1)
        if span.start == 0:
            keys = jnp.concatenate([nk_ref[:, mine], pad], axis=0)
            vals = jnp.concatenate([nv_ref[:, mine], pad], axis=0)
            s = jnp.where(seen, scores_of(queries[h], keys), NEG)
            m = jnp.broadcast_to(jnp.max(s, axis=1, keepdims=True), s.shape)
            p = jnp.where(seen, jnp.exp2((s - m) * LOG2_SCALE), 0.0).astype(bf16)
            vals = jnp.concatenate([vals, ones[:LANES]], axis=1)
            a = jnp.dot(p, vals, preferred_element_type=f32)
            acc = [a[r * ROW_BLOCK : (r + 1) * ROW_BLOCK] for r in range(chunks)]
            top = [m[r * ROW_BLOCK : (r + 1) * ROW_BLOCK] for r in range(chunks)]
        if h in copies:
            copies.pop(h).wait()
        vals = jnp.concatenate([values[h][span], ones], axis=1)
        for r in range(chunks):
            s = sb[n % 2][r * ROW_BLOCK : (r + 1) * ROW_BLOCK]
            m = jnp.maximum(top[r], jnp.max(s, axis=1, keepdims=True))
            p = jnp.exp2((s - jnp.tile(m, (1, KEY_BLOCK // LANES))) * LOG2_SCALE)
            decay = jnp.exp2((top[r] - m) * LOG2_SCALE)
            acc[r] = acc[r] * jnp.tile(decay, (1, 2)) + jnp.dot(
                p.astype(bf16), vals, preferred_element_type=f32
            )
            top[r] = m
        if span.stop == k_ref.shape[0]:
            whole, whole_top = jnp.concatenate(acc, axis=0), jnp.concatenate(top, axis=0)
            for g in range(2):
                slot = h * 2 + g
                part = whole[g * tokens : (g + 1) * tokens]
                part_top = whole_top[g * tokens : (g + 1) * tokens]
                o_ref[:dests, slot * own : (slot + 1) * own, :] = (
                    part[:, :HEAD].reshape(dests, own, HEAD).astype(bf16)
                )
                pick = lane == slot * own + at
                maxima = maxima + jnp.where(pick, part_top.reshape(dests, own, LANES), 0.0)
                sums = sums + jnp.where(pick, part[:, HEAD:].reshape(dests, own, LANES), 0.0)
    o_ref[:dests, 2 * kv_heads * own :, :] = packed_stats(
        jnp.sum(maxima, axis=1), jnp.sum(sums, axis=1)
    )


def attend(
    same_x, same_c, queries, keys, first, second, new_keys, new_values, fetch=False, carried=()
):
    (tokens, width), own = queries.shape, new_keys.shape[0]
    rows, prefix = 2 * tokens, keys.shape[0]
    whole = pl.BlockSpec(memory_space=pltpu.VMEM)
    specs = [whole] * 6
    specs += [whole] * len(carried)
    dests = (1 + len(carried)) * (tokens // own)
    outs = [jax.ShapeDtypeStruct((dests, width // HEAD * own + STATS, HEAD), bf16)]
    scratch = [pltpu.VMEM((rows, KEY_BLOCK), f32)] * 2
    if fetch:
        specs[3] = pl.BlockSpec(memory_space=pltpu.HBM)
        outs.append(jax.ShapeDtypeStruct(first.shape, first.dtype))
        scratch.append(pltpu.SemaphoreType.DMA((1,)))
        second = pltpu.with_memory_space_constraint(second, pltpu.HBM)
    return pl.pallas_call(
        functools.partial(attend_kernel, same_x, same_c),
        in_specs=specs,
        out_specs=[whole] * len(outs),
        out_shape=outs,
        scratch_shapes=scratch,
        compiler_params=pltpu.CompilerParams(vmem_limit_bytes=ATTEND_VMEM),
        cost_estimate=pl.CostEstimate(
            flops=4 * tokens * width * prefix,
            bytes_accessed=4 * prefix * keys.shape[1],
            transcendentals=tokens * width // HEAD * prefix,
        ),
        name="attend",
    )(queries, keys, first, second, new_keys, new_values, *carried)


def columns_of(rows):
    n = rows.shape[0]
    if n < LANES:
        rows = jnp.concatenate([rows, jnp.zeros((LANES - n, LANES), f32)], axis=0)
    return jnp.transpose(rows)


def merge_kernel(here_ref, there_ref, sib_ref, o_ref):
    n, pairs = here_ref.shape[0], here_ref.shape[1] - STATS
    x = lax.axis_index("xl")
    for column, a_ref, b_ref in (
        (x, here_ref, sib_ref.at[n:]),
        (1 - x, there_ref, sib_ref.at[:n]),
    ):
        ma, la = unpacked_stats(a_ref[:, pairs:, :])
        mb, lb = unpacked_stats(b_ref[:, pairs:, :])
        m = jnp.maximum(ma, mb)
        wa, wb = jnp.exp2((ma - m) * LOG2_SCALE), jnp.exp2((mb - m) * LOG2_SCALE)
        stats = packed_stats(m, la * wa + lb * wb)
        cols = columns_of(jnp.concatenate([wa, wb], axis=0))
        for d in range(n):
            slots = [RETURN_ORDER.index((k, Z_ORDER[d])) for k in range(2)]
            slot = jnp.where(column == 0, slots[0], slots[1])
            mixed = (
                a_ref[d, :pairs].astype(f32) * cols[:pairs, d : d + 1]
                + b_ref[d, :pairs].astype(f32) * cols[:pairs, n + d : n + d + 1]
            )
            o_ref[slot, :pairs] = mixed.astype(bf16)
            o_ref[slot, pairs:] = stats[d]


def merge(here, there, sibling):
    whole = pl.BlockSpec(memory_space=pltpu.VMEM)
    n, height, _ = here.shape
    return pl.pallas_call(
        merge_kernel,
        in_specs=[whole] * 3,
        out_specs=whole,
        out_shape=jax.ShapeDtypeStruct((2 * n, height, HEAD), bf16),
        compiler_params=pltpu.CompilerParams(vmem_limit_bytes=SMALL_VMEM),
        name="merge",
    )(here, there, sibling)


def finish_kernel(own, r_ref, o_ref):
    n, pairs = r_ref.shape[0], r_ref.shape[1] - STATS
    m, l = unpacked_stats(r_ref[:, pairs:, :])
    w = jnp.exp2((m - jnp.max(m, axis=0, keepdims=True)) * LOG2_SCALE)
    cols = columns_of(w / jnp.sum(l * w, axis=0, keepdims=True))
    out = r_ref[0, :pairs].astype(f32) * cols[:pairs, 0:1]
    for s in range(1, n):
        out = out + r_ref[s, :pairs].astype(f32) * cols[:pairs, s : s + 1]
    for j in range(pairs // own):
        o_ref[:, j * HEAD : (j + 1) * HEAD] = out[j * own : (j + 1) * own].astype(bf16)


def finish(received, own, width):
    whole = pl.BlockSpec(memory_space=pltpu.VMEM)
    return pl.pallas_call(
        functools.partial(finish_kernel, own),
        in_specs=[whole],
        out_specs=whole,
        out_shape=jax.ShapeDtypeStruct((own, width), bf16),
        compiler_params=pltpu.CompilerParams(vmem_limit_bytes=SMALL_VMEM),
        name="finish",
    )(received)


def exchanged(blocks, axes, order):
    return lax.all_to_all(
        blocks, axes, split_axis=0, concat_axis=0, tiled=True, axis_index_groups=[list(order)]
    )


def swapped(value, axis):
    return lax.ppermute(value, axis, [(0, 1), (1, 0)])


def after(value, earlier):
    return lax.optimization_barrier((value, earlier))[0]


def shards(queries, cache_keys, prefix_cache_values, incoming_keys, incoming_values):
    own, width = queries.shape
    column = lax.axis_size("z")
    local = loaded(cache_keys, prefix_cache_values, incoming_keys, incoming_values)
    here = exchanged(jnp.broadcast_to(queries, (column, own, width)), "z", Z_ORDER)
    here, *local = lax.optimization_barrier((here, *local))
    here = here.reshape(column * own, width)
    here_other = swapped(here, "c")
    there_other = lax.ppermute(here, ("xl", "c"), [(n, 3 - n) for n in range(4)])
    keys, first, *fresh = local
    part_here, second = attend(
        True, True, here, keys, first, prefix_cache_values, *fresh, fetch=True
    )
    local = (keys, first, second, *fresh)
    there = swapped(here, "xl")
    here_other, part_here = lax.optimization_barrier((here_other, part_here))
    (part_here_other,) = attend(True, False, here_other, *local)
    (part_others,) = attend(
        False, False, after(there_other, part_here_other), *local, carried=(part_here_other,)
    )
    part_others, there = lax.optimization_barrier((part_others, there))
    sibling = swapped(part_others, "c")
    (part_there,) = attend(False, True, there, *local)
    merged = merge(part_here, part_there, sibling)
    back = [x * column + z for x, z in RETURN_ORDER]
    return finish(exchanged(merged, ("xl", "z"), back), own, width)


def solution(mesh):
    fine = Mesh(mesh.devices.reshape(2, -1, 2, mesh.devices.shape[1]), ("xl", "z", "c", "head"))
    spec = P(("xl", "z", "c"), "head")
    return jax.shard_map(shards, mesh=fine, in_specs=(spec,) * 5, out_specs=spec, check_vma=False)
```

```python
import functools
import math

import jax
import jax.numpy as jnp
from jax import lax
from jax.experimental import pallas as pl
from jax.experimental.pallas import tpu as pltpu
from jax.sharding import Mesh
from jax.sharding import PartitionSpec as P

HEAD = 128
LANES = 128
LOG2_SCALE = 168.0**-0.5 * math.log2(math.e)
NEG = -1e30
KEY_BLOCK = 2048
ROW_BLOCK = 256
STATS = 8
PARTS = 4

Z_ORDER = (7, 3, 6, 2, 5, 1, 4, 0)
RETURN_ORDER = tuple((1 - x if z % 2 else x, z) for z in range(7, -1, -1) for x in range(2))

f32 = jnp.float32
bf16 = jnp.bfloat16

ATTEND_VMEM = 32 << 20
SMALL_VMEM = 4 << 20


def scores_of(a, b):
    return lax.dot_general(a, b, (((1,), (1,)), ((), ())), preferred_element_type=f32)


def split_three(value):
    high = value.astype(bf16)
    rest = value - high.astype(f32)
    middle = rest.astype(bf16)
    low = (rest - middle.astype(f32)).astype(bf16)
    return high.astype(f32), middle.astype(f32), low.astype(f32)


def packed_stats(m, l):
    pieces = (*split_three(m), *split_three(l))
    n = m.shape[0]
    row = lax.broadcasted_iota(jnp.int32, (n, STATS, LANES), 1)
    out = jnp.zeros((n, STATS, LANES), f32)
    for k, piece in enumerate(pieces):
        out = jnp.where(row == k, jnp.broadcast_to(piece[:, None, :], out.shape), out)
    return out.astype(bf16)


def unpacked_stats(stats):
    s = stats.astype(f32)
    m = (s[:, 2] + s[:, 1]) + s[:, 0]
    l = (s[:, 5] + s[:, 4]) + s[:, 3]
    return m, l


def load_kernel(k_ref, v_ref, nk_ref, nv_ref, k_out, v_out, nk_out, nv_out, sems):
    pairs = [(nk_ref, nk_out), (nv_ref, nv_out)]
    step = k_ref.shape[0] // PARTS
    for p in range(PARTS):
        span = pl.ds(p * step, step)
        pairs.append((k_ref.at[span], k_out.at[span]))
        pairs.append((v_ref.at[span, pl.ds(0, HEAD)], v_out.at[span]))
    copies = [
        pltpu.make_async_copy(source, target, sems.at[n])
        for n, (source, target) in enumerate(pairs)
    ]
    for copy in copies:
        copy.start()
    for copy in copies:
        copy.wait()


def loaded(keys, values, new_keys, new_values):
    arrays = (keys, values, new_keys, new_values)
    outs = [jax.ShapeDtypeStruct(a.shape, a.dtype) for a in arrays]
    outs[1] = jax.ShapeDtypeStruct((values.shape[0], HEAD), values.dtype)
    return pl.pallas_call(
        load_kernel,
        in_specs=[pl.BlockSpec(memory_space=pltpu.HBM)] * len(arrays),
        out_specs=[pl.BlockSpec(memory_space=pltpu.VMEM)] * len(arrays),
        out_shape=outs,
        scratch_shapes=[pltpu.SemaphoreType.DMA((2 * PARTS + 2,))],
        compiler_params=pltpu.CompilerParams(vmem_limit_bytes=SMALL_VMEM),
        cost_estimate=pl.CostEstimate(
            flops=0,
            bytes_accessed=sum(2 * a.size * a.dtype.itemsize for a in outs),
            transcendentals=0,
        ),
        name="load",
    )(*(pltpu.with_memory_space_constraint(a, pltpu.HBM) for a in arrays))


def attend_kernel(same_x, same_c, q_ref, k_ref, v0_ref, v1_ref, nk_ref, nv_ref, o_ref, *rest):
    copies = {}
    if len(rest) == 3:
        carried_ref, s0, s1 = (o_ref, *rest[1:])
        o_ref = rest[0]
        o_ref[o_ref.shape[0] // 2 :] = carried_ref[...]
    elif len(rest) > 2:
        v_hbm, (v1_ref, s0, s1, sems) = v1_ref, rest
        copies[1] = pltpu.make_async_copy(v_hbm.at[:, pl.ds(HEAD, HEAD)], v1_ref, sems.at[0])
        copies[1].start()
    else:
        s0, s1 = rest
    values = (v0_ref, v1_ref)
    tokens = q_ref.shape[0]
    own = nk_ref.shape[0]
    dests = tokens // own
    rows = 2 * tokens
    kv_heads = k_ref.shape[1] // HEAD
    chunks = rows // ROW_BLOCK
    x, z, c = lax.axis_index("xl"), lax.axis_index("z"), lax.axis_index("c")
    first = ((x * dests + z) * 2 + c) * own
    from_x, from_c = (x if same_x else 1 - x), (c if same_c else 1 - c)
    sb = (s0, s1)
    col = lax.broadcasted_iota(jnp.int32, (rows, LANES), 1)
    within = lax.broadcasted_iota(jnp.int32, (own, LANES), 0)
    position = jnp.concatenate(
        [((from_x * dests + z_from) * 2 + from_c) * own + within for z_from in Z_ORDER] * 2, axis=0
    )
    seen = (col < own) & (position >= first + col)
    at = lax.broadcasted_iota(jnp.int32, (dests, own, LANES), 1)
    lane = lax.broadcasted_iota(jnp.int32, (dests, own, LANES), 2)
    ones = jnp.ones((KEY_BLOCK, LANES), bf16)
    pad = jnp.zeros((LANES - own, HEAD), bf16)
    work = [
        (h, slice(start, start + KEY_BLOCK))
        for h in range(kv_heads)
        for start in range(0, k_ref.shape[0], KEY_BLOCK)
    ]
    queries = [
        jnp.concatenate(
            [q_ref[:, (2 * h + g) * HEAD : (2 * h + g + 1) * HEAD] for g in range(2)], axis=0
        )
        for h in range(kv_heads)
    ]

    def score_block(n):
        h, span = work[n]
        keys = k_ref[span, h * HEAD : (h + 1) * HEAD]
        sb[n % 2][...] = scores_of(queries[h], keys)

    score_block(0)
    maxima = jnp.zeros((dests, own, LANES), f32)
    sums = jnp.zeros((dests, own, LANES), f32)
    for n, (h, span) in enumerate(work):
        mine = slice(h * HEAD, (h + 1) * HEAD)
        if n + 1 < len(work):
            score_block(n + 1)
        if span.start == 0:
            keys = jnp.concatenate([nk_ref[:, mine], pad], axis=0)
            vals = jnp.concatenate([nv_ref[:, mine], pad], axis=0)
            s = jnp.where(seen, scores_of(queries[h], keys), NEG)
            m = jnp.broadcast_to(jnp.max(s, axis=1, keepdims=True), s.shape)
            p = jnp.where(seen, jnp.exp2((s - m) * LOG2_SCALE), 0.0).astype(bf16)
            vals = jnp.concatenate([vals, ones[:LANES]], axis=1)
            a = jnp.dot(p, vals, preferred_element_type=f32)
            acc = [a[r * ROW_BLOCK : (r + 1) * ROW_BLOCK] for r in range(chunks)]
            top = [m[r * ROW_BLOCK : (r + 1) * ROW_BLOCK] for r in range(chunks)]
        if h in copies:
            copies.pop(h).wait()
        vals = jnp.concatenate([values[h][span], ones], axis=1)
        for r in range(chunks):
            s = sb[n % 2][r * ROW_BLOCK : (r + 1) * ROW_BLOCK]
            m = jnp.maximum(top[r], jnp.max(s, axis=1, keepdims=True))
            p = jnp.exp2((s - jnp.tile(m, (1, KEY_BLOCK // LANES))) * LOG2_SCALE)
            decay = jnp.exp2((top[r] - m) * LOG2_SCALE)
            acc[r] = acc[r] * jnp.tile(decay, (1, 2)) + jnp.dot(
                p.astype(bf16), vals, preferred_element_type=f32
            )
            top[r] = m
        if span.stop == k_ref.shape[0]:
            whole, whole_top = jnp.concatenate(acc, axis=0), jnp.concatenate(top, axis=0)
            for g in range(2):
                slot = h * 2 + g
                part = whole[g * tokens : (g + 1) * tokens]
                part_top = whole_top[g * tokens : (g + 1) * tokens]
                o_ref[:dests, slot * own : (slot + 1) * own, :] = (
                    part[:, :HEAD].reshape(dests, own, HEAD).astype(bf16)
                )
                pick = lane == slot * own + at
                maxima = maxima + jnp.where(pick, part_top.reshape(dests, own, LANES), 0.0)
                sums = sums + jnp.where(pick, part[:, HEAD:].reshape(dests, own, LANES), 0.0)
    o_ref[:dests, 2 * kv_heads * own :, :] = packed_stats(
        jnp.sum(maxima, axis=1), jnp.sum(sums, axis=1)
    )


def attend(
    same_x, same_c, queries, keys, first, second, new_keys, new_values, fetch=False, carried=()
):
    (tokens, width), own = queries.shape, new_keys.shape[0]
    rows, prefix = 2 * tokens, keys.shape[0]
    whole = pl.BlockSpec(memory_space=pltpu.VMEM)
    specs = [whole] * 6
    specs += [whole] * len(carried)
    dests = (1 + len(carried)) * (tokens // own)
    outs = [jax.ShapeDtypeStruct((dests, width // HEAD * own + STATS, HEAD), bf16)]
    scratch = [pltpu.VMEM((rows, KEY_BLOCK), f32)] * 2
    if fetch:
        specs[3] = pl.BlockSpec(memory_space=pltpu.HBM)
        outs.append(jax.ShapeDtypeStruct(first.shape, first.dtype))
        scratch.append(pltpu.SemaphoreType.DMA((1,)))
        second = pltpu.with_memory_space_constraint(second, pltpu.HBM)
    return pl.pallas_call(
        functools.partial(attend_kernel, same_x, same_c),
        in_specs=specs,
        out_specs=[whole] * len(outs),
        out_shape=outs,
        scratch_shapes=scratch,
        compiler_params=pltpu.CompilerParams(vmem_limit_bytes=ATTEND_VMEM),
        cost_estimate=pl.CostEstimate(
            flops=4 * tokens * width * prefix,
            bytes_accessed=4 * prefix * keys.shape[1],
            transcendentals=tokens * width // HEAD * prefix,
        ),
        name="attend",
    )(queries, keys, first, second, new_keys, new_values, *carried)


def columns_of(rows):
    n = rows.shape[0]
    if n < LANES:
        rows = jnp.concatenate([rows, jnp.zeros((LANES - n, LANES), f32)], axis=0)
    return jnp.transpose(rows)


def merge_kernel(here_ref, there_ref, sib_ref, o_ref):
    n, pairs = here_ref.shape[0], here_ref.shape[1] - STATS
    x = lax.axis_index("xl")
    for column, a_ref, b_ref in (
        (x, here_ref, sib_ref.at[n:]),
        (1 - x, there_ref, sib_ref.at[:n]),
    ):
        ma, la = unpacked_stats(a_ref[:, pairs:, :])
        mb, lb = unpacked_stats(b_ref[:, pairs:, :])
        m = jnp.maximum(ma, mb)
        wa, wb = jnp.exp2((ma - m) * LOG2_SCALE), jnp.exp2((mb - m) * LOG2_SCALE)
        stats = packed_stats(m, la * wa + lb * wb)
        cols = columns_of(jnp.concatenate([wa, wb], axis=0))
        for d in range(n):
            slots = [RETURN_ORDER.index((k, Z_ORDER[d])) for k in range(2)]
            slot = jnp.where(column == 0, slots[0], slots[1])
            mixed = (
                a_ref[d, :pairs].astype(f32) * cols[:pairs, d : d + 1]
                + b_ref[d, :pairs].astype(f32) * cols[:pairs, n + d : n + d + 1]
            )
            o_ref[slot, :pairs] = mixed.astype(bf16)
            o_ref[slot, pairs:] = stats[d]


def merge(here, there, sibling):
    whole = pl.BlockSpec(memory_space=pltpu.VMEM)
    n, height, _ = here.shape
    return pl.pallas_call(
        merge_kernel,
        in_specs=[whole] * 3,
        out_specs=whole,
        out_shape=jax.ShapeDtypeStruct((2 * n, height, HEAD), bf16),
        compiler_params=pltpu.CompilerParams(vmem_limit_bytes=SMALL_VMEM),
        name="merge",
    )(here, there, sibling)


def finish_kernel(own, r_ref, o_ref):
    n, pairs = r_ref.shape[0], r_ref.shape[1] - STATS
    m, l = unpacked_stats(r_ref[:, pairs:, :])
    w = jnp.exp2((m - jnp.max(m, axis=0, keepdims=True)) * LOG2_SCALE)
    cols = columns_of(w / jnp.sum(l * w, axis=0, keepdims=True))
    out = r_ref[0, :pairs].astype(f32) * cols[:pairs, 0:1]
    for s in range(1, n):
        out = out + r_ref[s, :pairs].astype(f32) * cols[:pairs, s : s + 1]
    for j in range(pairs // own):
        o_ref[:, j * HEAD : (j + 1) * HEAD] = out[j * own : (j + 1) * own].astype(bf16)


def finish(received, own, width):
    whole = pl.BlockSpec(memory_space=pltpu.VMEM)
    return pl.pallas_call(
        functools.partial(finish_kernel, own),
        in_specs=[whole],
        out_specs=whole,
        out_shape=jax.ShapeDtypeStruct((own, width), bf16),
        compiler_params=pltpu.CompilerParams(vmem_limit_bytes=SMALL_VMEM),
        name="finish",
    )(received)


def exchanged(blocks, axes, order):
    return lax.all_to_all(
        blocks, axes, split_axis=0, concat_axis=0, tiled=True, axis_index_groups=[list(order)]
    )


def swapped(value, axis):
    return lax.ppermute(value, axis, [(0, 1), (1, 0)])


def after(value, earlier):
    return lax.optimization_barrier((value, earlier))[0]


def shards(queries, cache_keys, prefix_cache_values, incoming_keys, incoming_values):
    own, width = queries.shape
    column = lax.axis_size("z")
    local = loaded(cache_keys, prefix_cache_values, incoming_keys, incoming_values)
    here = exchanged(jnp.broadcast_to(queries, (column, own, width)), "z", Z_ORDER)
    here, *local = lax.optimization_barrier((here, *local))
    here = here.reshape(column * own, width)
    here_other = swapped(here, "c")
    there_other = lax.ppermute(here, ("xl", "c"), [(n, 3 - n) for n in range(4)])
    keys, first, *fresh = local
    part_here, second = attend(
        True, True, here, keys, first, prefix_cache_values, *fresh, fetch=True
    )
    local = (keys, first, second, *fresh)
    there = swapped(here, "xl")
    here_other, part_here = lax.optimization_barrier((here_other, part_here))
    (part_here_other,) = attend(True, False, here_other, *local)
    (part_others,) = attend(
        False, False, after(there_other, part_here_other), *local, carried=(part_here_other,)
    )
    part_others, there = lax.optimization_barrier((part_others, there))
    sibling = swapped(part_others, "c")
    (part_there,) = attend(False, True, there, *local)
    merged = merge(part_here, part_there, sibling)
    back = [x * column + z for x, z in RETURN_ORDER]
    return finish(exchanged(merged, ("xl", "z"), back), own, width)


def solution(mesh):
    fine = Mesh(mesh.devices.reshape(2, -1, 2, mesh.devices.shape[1]), ("xl", "z", "c", "head"))
    spec = P(("xl", "z", "c"), "head")
    return jax.shard_map(shards, mesh=fine, in_specs=(spec,) * 5, out_specs=spec, check_vma=False)
```

```python
import functools
import math

import jax
import jax.numpy as jnp
from jax import lax
from jax.experimental import pallas as pl
from jax.experimental.pallas import tpu as pltpu
from jax.sharding import Mesh
from jax.sharding import PartitionSpec as P

HEAD = 128
LANES = 128
LOG2_SCALE = 168.0**-0.5 * math.log2(math.e)
NEG = -1e30
KEY_BLOCK = 2048
ROW_BLOCK = 256
STATS = 8
PARTS = 4

Z_ORDER = (7, 5, 6, 4, 3, 1, 2, 0)
RETURN_ORDER = tuple((1 - x if z % 2 else x, z) for z in range(7, -1, -1) for x in range(2))

f32 = jnp.float32
bf16 = jnp.bfloat16

ATTEND_VMEM = 32 << 20
SMALL_VMEM = 4 << 20


def scores_of(a, b):
    return lax.dot_general(a, b, (((1,), (1,)), ((), ())), preferred_element_type=f32)


def split_three(value):
    high = value.astype(bf16)
    rest = value - high.astype(f32)
    middle = rest.astype(bf16)
    low = (rest - middle.astype(f32)).astype(bf16)
    return high.astype(f32), middle.astype(f32), low.astype(f32)


def packed_stats(m, l):
    pieces = (*split_three(m), *split_three(l))
    n = m.shape[0]
    row = lax.broadcasted_iota(jnp.int32, (n, STATS, LANES), 1)
    out = jnp.zeros((n, STATS, LANES), f32)
    for k, piece in enumerate(pieces):
        out = jnp.where(row == k, jnp.broadcast_to(piece[:, None, :], out.shape), out)
    return out.astype(bf16)


def unpacked_stats(stats):
    s = stats.astype(f32)
    m = (s[:, 2] + s[:, 1]) + s[:, 0]
    l = (s[:, 5] + s[:, 4]) + s[:, 3]
    return m, l


def load_kernel(k_ref, v_ref, nk_ref, nv_ref, k_out, v_out, nk_out, nv_out, sems):
    pairs = [(nk_ref, nk_out), (nv_ref, nv_out)]
    step = k_ref.shape[0] // PARTS
    for p in range(PARTS):
        span = pl.ds(p * step, step)
        pairs.append((k_ref.at[span], k_out.at[span]))
        pairs.append((v_ref.at[span, pl.ds(0, HEAD)], v_out.at[span]))
    copies = [
        pltpu.make_async_copy(source, target, sems.at[n])
        for n, (source, target) in enumerate(pairs)
    ]
    for copy in copies:
        copy.start()
    for copy in copies:
        copy.wait()


def loaded(keys, values, new_keys, new_values):
    arrays = (keys, values, new_keys, new_values)
    outs = [jax.ShapeDtypeStruct(a.shape, a.dtype) for a in arrays]
    outs[1] = jax.ShapeDtypeStruct((values.shape[0], HEAD), values.dtype)
    return pl.pallas_call(
        load_kernel,
        in_specs=[pl.BlockSpec(memory_space=pltpu.HBM)] * len(arrays),
        out_specs=[pl.BlockSpec(memory_space=pltpu.VMEM)] * len(arrays),
        out_shape=outs,
        scratch_shapes=[pltpu.SemaphoreType.DMA((2 * PARTS + 2,))],
        compiler_params=pltpu.CompilerParams(vmem_limit_bytes=SMALL_VMEM),
        cost_estimate=pl.CostEstimate(
            flops=0,
            bytes_accessed=sum(2 * a.size * a.dtype.itemsize for a in outs),
            transcendentals=0,
        ),
        name="load",
    )(*(pltpu.with_memory_space_constraint(a, pltpu.HBM) for a in arrays))


def attend_kernel(same_x, same_c, q_ref, k_ref, v0_ref, v1_ref, nk_ref, nv_ref, o_ref, *rest):
    copies = {}
    if len(rest) == 3:
        carried_ref, s0, s1 = (o_ref, *rest[1:])
        o_ref = rest[0]
        o_ref[o_ref.shape[0] // 2 :] = carried_ref[...]
    elif len(rest) > 2:
        v_hbm, (v1_ref, s0, s1, sems) = v1_ref, rest
        copies[1] = pltpu.make_async_copy(v_hbm.at[:, pl.ds(HEAD, HEAD)], v1_ref, sems.at[0])
        copies[1].start()
    else:
        s0, s1 = rest
    values = (v0_ref, v1_ref)
    tokens = q_ref.shape[0]
    own = nk_ref.shape[0]
    dests = tokens // own
    rows = 2 * tokens
    kv_heads = k_ref.shape[1] // HEAD
    chunks = rows // ROW_BLOCK
    x, z, c = lax.axis_index("xl"), lax.axis_index("z"), lax.axis_index("c")
    first = ((x * dests + z) * 2 + c) * own
    from_x, from_c = (x if same_x else 1 - x), (c if same_c else 1 - c)
    sb = (s0, s1)
    col = lax.broadcasted_iota(jnp.int32, (rows, LANES), 1)
    within = lax.broadcasted_iota(jnp.int32, (own, LANES), 0)
    position = jnp.concatenate(
        [((from_x * dests + z_from) * 2 + from_c) * own + within for z_from in Z_ORDER] * 2, axis=0
    )
    seen = (col < own) & (position >= first + col)
    at = lax.broadcasted_iota(jnp.int32, (dests, own, LANES), 1)
    lane = lax.broadcasted_iota(jnp.int32, (dests, own, LANES), 2)
    ones = jnp.ones((KEY_BLOCK, LANES), bf16)
    pad = jnp.zeros((LANES - own, HEAD), bf16)
    work = [
        (h, slice(start, start + KEY_BLOCK))
        for h in range(kv_heads)
        for start in range(0, k_ref.shape[0], KEY_BLOCK)
    ]
    queries = [
        jnp.concatenate(
            [q_ref[:, (2 * h + g) * HEAD : (2 * h + g + 1) * HEAD] for g in range(2)], axis=0
        )
        for h in range(kv_heads)
    ]

    def score_block(n):
        h, span = work[n]
        keys = k_ref[span, h * HEAD : (h + 1) * HEAD]
        sb[n % 2][...] = scores_of(queries[h], keys)

    score_block(0)
    maxima = jnp.zeros((dests, own, LANES), f32)
    sums = jnp.zeros((dests, own, LANES), f32)
    for n, (h, span) in enumerate(work):
        mine = slice(h * HEAD, (h + 1) * HEAD)
        if n + 1 < len(work):
            score_block(n + 1)
        if span.start == 0:
            keys = jnp.concatenate([nk_ref[:, mine], pad], axis=0)
            vals = jnp.concatenate([nv_ref[:, mine], pad], axis=0)
            s = jnp.where(seen, scores_of(queries[h], keys), NEG)
            m = jnp.broadcast_to(jnp.max(s, axis=1, keepdims=True), s.shape)
            p = jnp.where(seen, jnp.exp2((s - m) * LOG2_SCALE), 0.0).astype(bf16)
            vals = jnp.concatenate([vals, ones[:LANES]], axis=1)
            a = jnp.dot(p, vals, preferred_element_type=f32)
            acc = [a[r * ROW_BLOCK : (r + 1) * ROW_BLOCK] for r in range(chunks)]
            top = [m[r * ROW_BLOCK : (r + 1) * ROW_BLOCK] for r in range(chunks)]
        if h in copies:
            copies.pop(h).wait()
        vals = jnp.concatenate([values[h][span], ones], axis=1)
        for r in range(chunks):
            s = sb[n % 2][r * ROW_BLOCK : (r + 1) * ROW_BLOCK]
            m = jnp.maximum(top[r], jnp.max(s, axis=1, keepdims=True))
            p = jnp.exp2((s - jnp.tile(m, (1, KEY_BLOCK // LANES))) * LOG2_SCALE)
            decay = jnp.exp2((top[r] - m) * LOG2_SCALE)
            acc[r] = acc[r] * jnp.tile(decay, (1, 2)) + jnp.dot(
                p.astype(bf16), vals, preferred_element_type=f32
            )
            top[r] = m
        if span.stop == k_ref.shape[0]:
            whole, whole_top = jnp.concatenate(acc, axis=0), jnp.concatenate(top, axis=0)
            for g in range(2):
                slot = h * 2 + g
                part = whole[g * tokens : (g + 1) * tokens]
                part_top = whole_top[g * tokens : (g + 1) * tokens]
                o_ref[:dests, slot * own : (slot + 1) * own, :] = (
                    part[:, :HEAD].reshape(dests, own, HEAD).astype(bf16)
                )
                pick = lane == slot * own + at
                maxima = maxima + jnp.where(pick, part_top.reshape(dests, own, LANES), 0.0)
                sums = sums + jnp.where(pick, part[:, HEAD:].reshape(dests, own, LANES), 0.0)
    o_ref[:dests, 2 * kv_heads * own :, :] = packed_stats(
        jnp.sum(maxima, axis=1), jnp.sum(sums, axis=1)
    )


def attend(
    same_x, same_c, queries, keys, first, second, new_keys, new_values, fetch=False, carried=()
):
    (tokens, width), own = queries.shape, new_keys.shape[0]
    rows, prefix = 2 * tokens, keys.shape[0]
    whole = pl.BlockSpec(memory_space=pltpu.VMEM)
    specs = [whole] * 6
    specs += [whole] * len(carried)
    dests = (1 + len(carried)) * (tokens // own)
    outs = [jax.ShapeDtypeStruct((dests, width // HEAD * own + STATS, HEAD), bf16)]
    scratch = [pltpu.VMEM((rows, KEY_BLOCK), f32)] * 2
    if fetch:
        specs[3] = pl.BlockSpec(memory_space=pltpu.HBM)
        outs.append(jax.ShapeDtypeStruct(first.shape, first.dtype))
        scratch.append(pltpu.SemaphoreType.DMA((1,)))
        second = pltpu.with_memory_space_constraint(second, pltpu.HBM)
    return pl.pallas_call(
        functools.partial(attend_kernel, same_x, same_c),
        in_specs=specs,
        out_specs=[whole] * len(outs),
        out_shape=outs,
        scratch_shapes=scratch,
        compiler_params=pltpu.CompilerParams(vmem_limit_bytes=ATTEND_VMEM),
        cost_estimate=pl.CostEstimate(
            flops=4 * tokens * width * prefix,
            bytes_accessed=4 * prefix * keys.shape[1],
            transcendentals=tokens * width // HEAD * prefix,
        ),
        name="attend",
    )(queries, keys, first, second, new_keys, new_values, *carried)


def columns_of(rows):
    n = rows.shape[0]
    if n < LANES:
        rows = jnp.concatenate([rows, jnp.zeros((LANES - n, LANES), f32)], axis=0)
    return jnp.transpose(rows)


def merge_kernel(here_ref, there_ref, sib_ref, o_ref):
    n, pairs = here_ref.shape[0], here_ref.shape[1] - STATS
    x = lax.axis_index("xl")
    for column, a_ref, b_ref in (
        (x, here_ref, sib_ref.at[n:]),
        (1 - x, there_ref, sib_ref.at[:n]),
    ):
        ma, la = unpacked_stats(a_ref[:, pairs:, :])
        mb, lb = unpacked_stats(b_ref[:, pairs:, :])
        m = jnp.maximum(ma, mb)
        wa, wb = jnp.exp2((ma - m) * LOG2_SCALE), jnp.exp2((mb - m) * LOG2_SCALE)
        stats = packed_stats(m, la * wa + lb * wb)
        cols = columns_of(jnp.concatenate([wa, wb], axis=0))
        for d in range(n):
            slots = [RETURN_ORDER.index((k, Z_ORDER[d])) for k in range(2)]
            slot = jnp.where(column == 0, slots[0], slots[1])
            mixed = (
                a_ref[d, :pairs].astype(f32) * cols[:pairs, d : d + 1]
                + b_ref[d, :pairs].astype(f32) * cols[:pairs, n + d : n + d + 1]
            )
            o_ref[slot, :pairs] = mixed.astype(bf16)
            o_ref[slot, pairs:] = stats[d]


def merge(here, there, sibling):
    whole = pl.BlockSpec(memory_space=pltpu.VMEM)
    n, height, _ = here.shape
    return pl.pallas_call(
        merge_kernel,
        in_specs=[whole] * 3,
        out_specs=whole,
        out_shape=jax.ShapeDtypeStruct((2 * n, height, HEAD), bf16),
        compiler_params=pltpu.CompilerParams(vmem_limit_bytes=SMALL_VMEM),
        name="merge",
    )(here, there, sibling)


def finish_kernel(own, r_ref, o_ref):
    n, pairs = r_ref.shape[0], r_ref.shape[1] - STATS
    m, l = unpacked_stats(r_ref[:, pairs:, :])
    w = jnp.exp2((m - jnp.max(m, axis=0, keepdims=True)) * LOG2_SCALE)
    cols = columns_of(w / jnp.sum(l * w, axis=0, keepdims=True))
    out = r_ref[0, :pairs].astype(f32) * cols[:pairs, 0:1]
    for s in range(1, n):
        out = out + r_ref[s, :pairs].astype(f32) * cols[:pairs, s : s + 1]
    for j in range(pairs // own):
        o_ref[:, j * HEAD : (j + 1) * HEAD] = out[j * own : (j + 1) * own].astype(bf16)


def finish(received, own, width):
    whole = pl.BlockSpec(memory_space=pltpu.VMEM)
    return pl.pallas_call(
        functools.partial(finish_kernel, own),
        in_specs=[whole],
        out_specs=whole,
        out_shape=jax.ShapeDtypeStruct((own, width), bf16),
        compiler_params=pltpu.CompilerParams(vmem_limit_bytes=SMALL_VMEM),
        name="finish",
    )(received)


def exchanged(blocks, axes, order):
    return lax.all_to_all(
        blocks, axes, split_axis=0, concat_axis=0, tiled=True, axis_index_groups=[list(order)]
    )


def swapped(value, axis):
    return lax.ppermute(value, axis, [(0, 1), (1, 0)])


def after(value, earlier):
    return lax.optimization_barrier((value, earlier))[0]


def shards(queries, cache_keys, prefix_cache_values, incoming_keys, incoming_values):
    own, width = queries.shape
    column = lax.axis_size("z")
    local = loaded(cache_keys, prefix_cache_values, incoming_keys, incoming_values)
    here = exchanged(jnp.broadcast_to(queries, (column, own, width)), "z", Z_ORDER)
    here, *local = lax.optimization_barrier((here, *local))
    here = here.reshape(column * own, width)
    here_other = swapped(here, "c")
    there_other = lax.ppermute(here, ("xl", "c"), [(n, 3 - n) for n in range(4)])
    keys, first, *fresh = local
    part_here, second = attend(
        True, True, here, keys, first, prefix_cache_values, *fresh, fetch=True
    )
    local = (keys, first, second, *fresh)
    there = swapped(here, "xl")
    here_other, part_here = lax.optimization_barrier((here_other, part_here))
    (part_here_other,) = attend(True, False, here_other, *local)
    (part_others,) = attend(
        False, False, after(there_other, part_here_other), *local, carried=(part_here_other,)
    )
    part_others, there = lax.optimization_barrier((part_others, there))
    sibling = swapped(part_others, "c")
    (part_there,) = attend(False, True, there, *local)
    merged = merge(part_here, part_there, sibling)
    back = [x * column + z for x, z in RETURN_ORDER]
    return finish(exchanged(merged, ("xl", "z"), back), own, width)


def solution(mesh):
    fine = Mesh(mesh.devices.reshape(2, -1, 2, mesh.devices.shape[1]), ("xl", "z", "c", "head"))
    spec = P(("xl", "z", "c"), "head")
    return jax.shard_map(shards, mesh=fine, in_specs=(spec,) * 5, out_specs=spec, check_vma=False)
```
